128 devices in a mesh: ao: 8 (over z, core), mo: 16 (over x, y).
Axes of the slice: x: 4, y: 4, z: 4, core: 2. Of those that a mesh axis runs over, the one named last changes fastest.
Arguments:
- pair_ints: bfloat16 [128, 4096, 256], P(('ao', 'mo')), may hold values from -6 to 6
- shell_pairs: int32 [128, 2], replicated, may hold values from 0 to 31, as said below
- occ_lam: bfloat16 [16, 32], replicated, may hold values from -1.5 to 1.5
- occ_sig: bfloat16 [16, 8], replicated, may hold values from -1.5 to 1.5
- coef_act: bfloat16 [2048, 2048], P(None, 'mo'), may hold values from -0.1875 to 0.1875
- slabs: int32 [2], replicated, may hold values from 0 to 7, as said below
Outputs:
- mo_ints: bfloat16 [2, 8, 4, 2048, 2048], P(None, 'ao', None, 'mo')
The draws below stay inside these ranges and needn't reach their ends.
Inputs may be any that keep to these rules, and one draw needn't show every extreme that they name: `shell_pairs`: each row holds two shell numbers P <= Q, no two rows are equal, and some row holds 0 and 31. `slabs`: the two slab numbers differ.
All inputs are finite; a program needn't handle non-finite values.
Results may differ from the reference program's by a relative error of at most 0.0066.
Values may be sent and summed in bfloat16 or wider, within the bound.
No kernel may reach another device: no remote copies, remote signals or barrier semaphores. Data moves between devices by JAX's collectives and lax.ppermute only.
A program may use at most 128 MiB of HBM per device.

```python
import jax
import jax.numpy as jnp
from jax import lax

SH = 64
NSH = 32
NAO = 2048
ACT = 2048
KL = 16
KS = 16
NI = 4
NSLAB = 8
NOCC = 32
NJ = 8
NBLK = 128


def draw_shell_pairs(key, part):
    first_shell, second_shell = jnp.triu_indices(NSH)
    pair_count = NSH * (NSH + 1) // 2
    corner_index = NSH - 1
    shuffled = jax.random.permutation(jax.random.fold_in(key, 11), pair_count - 1).astype(jnp.int32)
    shuffled = jnp.where(shuffled >= corner_index, shuffled + 1, shuffled)
    chosen = jnp.concatenate([jnp.full((1,), corner_index, jnp.int32), shuffled[:NBLK - 1]])
    reorder = jax.random.permutation(jax.random.fold_in(key, 12), NBLK)
    chosen = chosen[reorder]
    shell_one = jnp.asarray(first_shell, jnp.int32)[chosen]
    shell_two = jnp.asarray(second_shell, jnp.int32)[chosen]
    return jnp.stack([shell_one, shell_two], axis=1).astype(jnp.int32)


def draw_slabs(key, part):
    other_slab = jax.random.randint(jax.random.fold_in(key, 21), (), 0, NSLAB - 1).astype(jnp.int32)
    flipped = jax.random.randint(jax.random.fold_in(key, 22), (), 0, 2).astype(jnp.int32)
    last_slab = jnp.full((), NSLAB - 1, jnp.int32)
    first_value = jnp.where(flipped == 0, other_slab, last_slab)
    second_value = jnp.where(flipped == 0, last_slab, other_slab)
    return jnp.stack([first_value, second_value]).astype(jnp.int32)


def block_scale(rng, dims, cuts, least, largest):
    gain = 1.0
    for dim, blocks in cuts:
        draws = jax.random.uniform(jax.random.fold_in(jax.random.fold_in(rng, 6), dim), (blocks,), jnp.float32, least / len(cuts), largest / len(cuts))
        gain = gain * jnp.repeat(jnp.exp(draws), dims[dim] // blocks).reshape((-1,) + (1,) * (len(dims) - 1 - dim))
    return gain


def gaussian(key, dims, scale, bound, shards=(), held_as=jnp.bfloat16):
    result = scale * jax.random.normal(key, dims, jnp.float32)
    if shards:
        result = result * block_scale(key, dims, shards, -0.22, 0.18)
    return jnp.clip(result, -bound, bound).astype(held_as)


def setup_inputs(seed: int = 0) -> dict:
    keys = jax.random.split(jax.random.key(seed), 7)
    pair_ints = gaussian(keys[0], (NBLK, SH * SH, KL * KS), 1.0, 6.0, ((0, 128),))
    shell_pairs = draw_shell_pairs(jax.random.fold_in(keys[6], 71), 0)
    occ_lam = gaussian(keys[2], (KL, NOCC), KL ** -0.5, 1.5)
    occ_sig = gaussian(keys[3], (KS, NJ), KS ** -0.5, 1.5)
    coef_act = gaussian(keys[4], (NAO, ACT), (SH * 16) ** -0.5, 0.1875, ((1, 16),))
    slabs = draw_slabs(jax.random.fold_in(keys[6], 71), 0)
    return dict(pair_ints=pair_ints, shell_pairs=shell_pairs, occ_lam=occ_lam, occ_sig=occ_sig, coef_act=coef_act, slabs=slabs)


def one_slab(pair_ints, shell_pairs, occ_lam, occ_sig, coef_act, slab_index):
    lam_cols = lax.dynamic_slice_in_dim(occ_lam.astype(jnp.float32), slab_index * NI, NI, 1)
    pair_coef = occ_sig.astype(jnp.float32).T[:, None, None, :] * lam_cols.T[None, :, :, None]
    pair_coef = pair_coef.reshape(NJ * NI, KL * KS).astype(jnp.bfloat16)
    half_ints = jnp.dot(pair_ints.reshape(NBLK * SH * SH, KL * KS), pair_coef.T, preferred_element_type=jnp.float32)
    half_ints = half_ints.astype(jnp.bfloat16).reshape(NBLK, SH, SH, NJ, NI)
    per_orbital = jnp.moveaxis(half_ints, 3, 0)
    coef_shells = coef_act.astype(jnp.float32).reshape(NSH, SH, ACT)

    def per_occupied(orbital_blocks):
        def add_block(left_terms, block_item):
            block_vals, block_pair = block_item
            shell_one = block_pair[0]
            shell_two = block_pair[1]
            values = block_vals.astype(jnp.float32)
            term_one = jnp.einsum('mni,ma->ian', values, coef_shells[shell_one])
            differs = (shell_one != shell_two).astype(jnp.float32)
            term_two = jnp.einsum('mni,na->iam', values, coef_shells[shell_two]) * differs
            left_terms = left_terms.at[:, :, shell_two].add(term_one)
            left_terms = left_terms.at[:, :, shell_one].add(term_two)
            return left_terms, None

        start_terms = jnp.zeros((NI, ACT, NSH, SH), jnp.float32)
        left_terms = lax.scan(add_block, start_terms, (orbital_blocks, shell_pairs))[0]
        left_rounded = left_terms.astype(jnp.bfloat16).reshape(NI * ACT, NAO)
        product = jnp.dot(left_rounded, coef_act, preferred_element_type=jnp.float32)
        return product.astype(jnp.bfloat16).reshape(NI, ACT, ACT)

    return lax.map(per_occupied, per_orbital)


def reference(pair_ints, shell_pairs, occ_lam, occ_sig, coef_act, slabs):
    first_slab = one_slab(pair_ints, shell_pairs, occ_lam, occ_sig, coef_act, slabs[0])
    second_slab = one_slab(pair_ints, shell_pairs, occ_lam, occ_sig, coef_act, slabs[1])
    return jnp.stack([first_slab, second_slab])
```

```python
import functools

import jax
import jax.numpy as jnp
from jax import lax
from jax.experimental import pallas as pl
from jax.experimental.pallas import tpu as pltpu
from jax.sharding import PartitionSpec as P

SH = 64
NSH = 32
NAO = 2048
ACT = 2048
KL = 16
KS = 16
NI = 4
NJ = 8
PANEL = 128
ROWS = NI * PANEL
AXES = ("ao", "mo")
OFFSETS = (0, 3, 1, 2)


def device_pairs(move):
    pairs = []
    for z in range(4):
        for c in range(2):
            for x in range(4):
                for y in range(4):
                    x2, y2, z2, c2 = move(x, y, z, c)
                    source = (z * 2 + c) * 16 + x * 4 + y
                    target = ((z2 % 4) * 2 + c2) * 16 + (x2 % 4) * 4 + y2 % 4
                    pairs.append((source, target))
    return pairs


def plane_pairs(step, phase):
    return device_pairs(
        lambda x, y, z, c: (x + step, y, z, c) if c == phase else (x, y + step, z, c)
    )


def z_pairs(step):
    return device_pairs(lambda x, y, z, c: (x, y, z + step, c))


def send(value, pairs):
    return lax.ppermute(value, AXES, pairs)


def ring(value, pairs_up, pairs_down, axis):
    half = value.shape[axis] // 2
    from_left = send(value, pairs_up)
    from_right = send(value, pairs_down)
    far_first = send(lax.slice_in_dim(from_left, 0, half, axis=axis), pairs_up)
    far_second = send(lax.slice_in_dim(from_right, half, 2 * half, axis=axis), pairs_down)
    return value, from_left, from_right, far_first, far_second


def plane_ring(value, phase, axis):
    return ring(value, plane_pairs(1, phase), plane_pairs(-1, phase), axis)


def gather_coefs(chunk):
    own, left, right, far_a, far_b = plane_ring(chunk[None], 0, 1)
    row = jnp.concatenate([own, left, right, jnp.concatenate([far_a, far_b], axis=1)], axis=0)
    whole = jnp.concatenate(plane_ring(row, 1, 0), axis=0)
    column = ring(whole, z_pairs(1), z_pairs(-1), 0)
    swap = device_pairs(lambda x, y, z, c: (x, y, z, 1 - c))
    return list(column), [send(piece, swap) for piece in column]


def slab_kernel(slab, n_in, *refs):
    pairs_ref, place_ref = refs[:2]
    halves = refs[2:7]
    coefs_own = refs[7:12]
    coefs_other = refs[12:17]
    lhs_hbm = refs[17]
    (out_ref, blocks, coefs, lhs, acc_one, acc_two, left, staged, sem_blocks, sem_coefs,
     sem_lhs, sem_out) = refs[n_in:]
    x = place_ref[0]
    y = place_ref[1]
    z = place_ref[2]
    core = place_ref[3]

    def source(slot, which_core):
        first = jnp.where(which_core == 0, x, y)
        second = jnp.where(which_core == 0, y, x)
        inner = slot % 4
        outer = slot // 4
        if isinstance(slot, int):
            first = (first + OFFSETS[inner]) & 3
            second = (second + OFFSETS[outer]) & 3
        else:
            first = (first + jnp.where(inner == 0, 0, jnp.where(inner == 3, 2, (inner * 2 + 1) & 3))) & 3
            second = (second + jnp.where(outer == 0, 0, jnp.where(outer == 3, 2, (outer * 2 + 1) & 3))) & 3
        return jnp.where(which_core == 0, first * 4 + second, second * 4 + first)

    copy_lhs = pltpu.make_async_copy(lhs_hbm, lhs, sem_lhs)
    copy_lhs.start()
    starts = (0, 32, 64, 96, 112, 128)
    copies = [
        pltpu.make_async_copy(
            halves[i], blocks.at[pl.ds(starts[i], starts[i + 1] - starts[i])], sem_blocks.at[i]
        )
        for i in range(5)
    ]
    for copy in copies:
        copy.start()
    for pieces, which_core in ((coefs_own, core), (coefs_other, 1 - core)):
        for piece, offset, slots, base in (
            (pieces[0], 0, 16, 0), (pieces[1], 3, 16, 0), (pieces[2], 1, 16, 0),
            (pieces[3], 2, 8, 0), (pieces[4], 2, 8, 8),
        ):
            row = pl.multiple_of((((z + offset) & 3) * 2 + which_core) * 256, 256)
            for s in range(slots):
                pltpu.make_async_copy(
                    piece.at[s],
                    coefs.at[source(base + s, which_core), pl.ds(row, 256)],
                    sem_coefs,
                ).start()

    @pl.loop(0, NSH)
    def _(shell):
        acc_one[shell] = jnp.zeros(acc_one.shape[1:], jnp.float32)
        acc_two[shell] = jnp.zeros(acc_two.shape[1:], jnp.float32)

    copy_lhs.wait()

    def add_group(group):
        came_from = source(group, core)
        for i in range(8):
            p = i * 16 + came_from
            one = pairs_ref[2 * p]
            two = pairs_ref[2 * p + 1]
            block = blocks[group * 8 + i]
            term_one = jnp.dot(
                lhs[one, 0:PANEL, 0:SH], block, preferred_element_type=jnp.float32
            )
            stacked = jnp.concatenate([block[:, 0:128], block[:, 128:256]], axis=0)
            term_two = lax.dot_general(
                lhs[two], stacked, (((1,), (1,)), ((), ())), preferred_element_type=jnp.float32
            )
            acc_one[two] += term_one
            spare = jnp.where(one == two, NSH, one)
            acc_two[spare] += term_two

    for i in range(5):
        copies[i].wait()

        @pl.loop(starts[i] // 8, starts[i + 1] // 8)
        def _(group):
            add_group(group)

    low = lax.broadcasted_iota(jnp.int32, (PANEL, 128), 1) < SH

    @pl.loop(0, NSH // 2)
    def _(t):
        for rp in range(2):
            one_a = acc_one[2 * t, :, rp * 128:rp * 128 + 128]
            one_b = acc_one[2 * t + 1, :, rp * 128:rp * 128 + 128]
            for r01 in range(2):
                two_a = acc_two[2 * t, r01 * PANEL:(r01 + 1) * PANEL, :]
                two_b = acc_two[2 * t + 1, r01 * PANEL:(r01 + 1) * PANEL, :]
                if r01 == 0:
                    part = jnp.where(low, one_a, pltpu.roll(one_b, SH, 1))
                else:
                    part = jnp.where(low, pltpu.roll(one_a, SH, 1), one_b)
                if rp == 0:
                    part += jnp.where(low, two_a, pltpu.roll(two_b, SH, 1))
                else:
                    part += jnp.where(low, pltpu.roll(two_a, SH, 1), two_b)
                r = rp * 2 + r01
                left[r * PANEL:(r + 1) * PANEL, pl.ds(pl.multiple_of(t * 128, 128), 128)] = (
                    part.astype(jnp.bfloat16)
                )

    pltpu.make_async_copy(coefs, coefs, sem_coefs).wait()

    def out_copy(n, slot):
        return pltpu.make_async_copy(
            staged.at[slot],
            out_ref.at[slab, :, pl.ds(pl.multiple_of(n * 256, 256), 256)],
            sem_out.at[slot],
        )

    @pl.loop(0, ACT // 256)
    def _(n):
        slot = n % 2

        @pl.when(n >= 2)
        def _():
            out_copy(n - 2, slot).wait()

        rhs = jnp.concatenate([coefs[2 * n], coefs[2 * n + 1]], axis=1)
        for h in range(2):
            product = jnp.dot(
                left[h * 256:(h + 1) * 256, :], rhs, preferred_element_type=jnp.float32
            )
            staged[slot, h * 256:(h + 1) * 256, :] = product.astype(jnp.bfloat16)
        out_copy(n, slot).start()

    out_copy(ACT // 256 - 2, 0).wait()
    out_copy(ACT // 256 - 1, 1).wait()


def finish_slab(slab, pairs, place, halves, coefs_own, coefs_other, lhs, previous):
    operands = [pairs, place, *halves, *coefs_own, *coefs_other, lhs]
    specs = [pl.BlockSpec(memory_space=pltpu.SMEM)] * 2
    specs += [pl.BlockSpec(memory_space=pl.ANY)] * (len(operands) - 2)
    aliases = {}
    if previous is not None:
        aliases = {len(operands): 0}
        operands.append(previous)
        specs.append(pl.BlockSpec(memory_space=pl.ANY))
    return pl.pallas_call(
        functools.partial(slab_kernel, slab, len(operands)),
        out_shape=jax.ShapeDtypeStruct((2, ROWS, ACT), jnp.bfloat16),
        in_specs=specs,
        out_specs=pl.BlockSpec(memory_space=pl.ANY),
        scratch_shapes=[
            pltpu.VMEM((128, SH, NI * SH), jnp.bfloat16),
            pltpu.VMEM((16, NAO, PANEL), jnp.bfloat16),
            pltpu.VMEM((NSH, 2 * PANEL, 2 * SH), jnp.bfloat16),
            pltpu.VMEM((NSH, PANEL, NI * SH), jnp.float32),
            pltpu.VMEM((NSH + 1, 2 * PANEL, 2 * SH), jnp.float32),
            pltpu.VMEM((ROWS, NAO), jnp.bfloat16),
            pltpu.VMEM((2, ROWS, 256), jnp.bfloat16),
            pltpu.SemaphoreType.DMA((5,)),
            pltpu.SemaphoreType.DMA,
            pltpu.SemaphoreType.DMA,
            pltpu.SemaphoreType.DMA((2,)),
        ],
        input_output_aliases=aliases,
        compiler_params=pltpu.CompilerParams(vmem_limit_bytes=48 << 20),
        cost_estimate=pl.CostEstimate(
            flops=9_000_000_000, bytes_accessed=18_000_000, transcendentals=0
        ),
        name="finish_slab",
    )(*operands)


def body(pair_ints, shell_pairs, occ_lam, occ_sig, coef_act, slabs):
    ao_index = lax.axis_index("ao")
    mo_index = lax.axis_index("mo")
    place = jnp.stack([mo_index // 4, mo_index % 4, ao_index // 2, ao_index % 2]).astype(jnp.int32)
    chunk = lax.dynamic_slice_in_dim(coef_act, ao_index * 256, 256, 0)
    coefs_own, coefs_other = gather_coefs(chunk)

    lam = occ_lam.astype(jnp.float32).reshape(KL, -1, NI)
    lam = jnp.take(lam, slabs, axis=1)
    pair_coef = occ_sig.astype(jnp.float32).T[:, None, None, None, :] * lam.transpose(1, 2, 0)[None, :, :, :, None]
    pair_coef = pair_coef.reshape(NJ * 2 * NI, KL * KS).astype(jnp.bfloat16)
    half = jnp.dot(pair_coef, pair_ints[0].T, preferred_element_type=jnp.float32).astype(jnp.bfloat16)
    half = half.reshape(NJ, 2, NI, SH, SH).transpose(0, 1, 3, 2, 4).reshape(NJ, 2, SH, NI * SH)
    owned = lax.all_to_all(half, "ao", split_axis=0, concat_axis=0, tiled=True)
    near = plane_ring(owned, 0, 0)
    rows = [jnp.concatenate([piece[:, k] for piece in near], axis=0) for k in range(2)]

    coef_t = coef_act.T.reshape(PANEL, NSH, SH).transpose(1, 0, 2)
    nothing = jnp.zeros_like(coef_t)
    lhs = jnp.concatenate(
        [jnp.concatenate([coef_t, nothing], axis=2), jnp.concatenate([nothing, coef_t], axis=2)], axis=1
    )
    pairs = shell_pairs.reshape(-1)
    out = None
    for k in range(2):
        halves = plane_ring(rows[k], 1, 0)
        out = finish_slab(k, pairs, place, halves, coefs_own, coefs_other, lhs, out)
    return out.reshape(2, 1, NI, PANEL, ACT)


def solution(mesh):
    return jax.shard_map(
        body,
        mesh=mesh,
        in_specs=(P(("ao", "mo"), None, None), P(), P(), P(), P(None, "mo"), P()),
        out_specs=P(None, "ao", None, "mo", None),
        check_vma=False,
    )
```

```python
import functools

import jax
import jax.numpy as jnp
from jax import lax
from jax.experimental import pallas as pl
from jax.experimental.pallas import tpu as pltpu
from jax.sharding import PartitionSpec as P

SH = 64
NSH = 32
NAO = 2048
ACT = 2048
KL = 16
KS = 16
NI = 4
NJ = 8
NOCC = 32
NBLK = 128
PANEL = 128
ROWS = NI * PANEL
VMEM_LIMIT = 60 << 20
AXES = ("ao", "mo")


def device_pairs(move):
    pairs = []
    for z in range(4):
        for c in range(2):
            for x in range(4):
                for y in range(4):
                    x2, y2, z2, c2 = move(x, y, z, c)
                    source = (z * 2 + c) * 16 + x * 4 + y
                    target = ((z2 % 4) * 2 + c2) * 16 + (x2 % 4) * 4 + y2 % 4
                    pairs.append((source, target))
    return pairs


def plane_pairs(step, phase):
    return device_pairs(
        lambda x, y, z, c: (x + step, y, z, c) if c == phase else (x, y + step, z, c)
    )


def z_pairs(step):
    return device_pairs(lambda x, y, z, c: (x, y, z + step, c))


def send(value, pairs):
    return lax.ppermute(value, AXES, pairs)


def after(value, *others):
    return lax.optimization_barrier((value, *others))[0]


def both_ways(value, pairs_up, pairs_down):
    return value, send(value, pairs_up), send(value, pairs_down)


def far_halves(pieces, pairs_up, pairs_down, *others):
    half = pieces[0].shape[0] // 2
    return (
        send(after(pieces[1], *others)[:half], pairs_up),
        send(after(pieces[2], *others)[half:], pairs_down),
    )


def direct(value, phase):
    return [value] + [send(value, plane_pairs(step, phase)) for step in (1, -1, 2)]


def ket_kernel(slabs_ref, lam_ref, sig_ref, ints_hbm, out_ref, ints, wide, sems):
    copies = [
        pltpu.make_async_copy(
            ints_hbm.at[0, pl.ds(n * 1024, 1024)], ints.at[pl.ds(n * 1024, 1024)], sems.at[n]
        )
        for n in range(4)
    ]
    for copy in copies:
        copy.start()
    rows = lax.broadcasted_iota(jnp.int32, (64, NOCC), 0)
    column = lax.broadcasted_iota(jnp.int32, (64, NOCC), 1)
    number = jnp.where((rows & 1) == 0, slabs_ref[0], slabs_ref[1]) * NI + (rows >> 4)
    pick_lam = jnp.where(column == number, 1.0, 0.0).astype(jnp.bfloat16)
    rows = lax.broadcasted_iota(jnp.int32, (64, NJ), 0)
    column = lax.broadcasted_iota(jnp.int32, (64, NJ), 1)
    pick_sig = jnp.where(column == ((rows >> 1) & 7), 1.0, 0.0).astype(jnp.bfloat16)
    line = lax.broadcasted_iota(jnp.int32, (KL, KL * KS), 0)
    word = lax.broadcasted_iota(jnp.int32, (KL, KL * KS), 1)
    spread_lam = jnp.where((word >> 4) == line, 1.0, 0.0).astype(jnp.bfloat16)
    spread_sig = jnp.where((word & 15) == line, 1.0, 0.0).astype(jnp.bfloat16)

    few_lam = lax.dot_general(
        pick_lam, lam_ref[...], (((1,), (1,)), ((), ())), preferred_element_type=jnp.float32
    )
    few_sig = jnp.dot(pick_sig, sig_ref[...], preferred_element_type=jnp.float32)

    def spread_out(few, spread):
        return jnp.dot(few.astype(jnp.bfloat16), spread, preferred_element_type=jnp.float32)

    pair_coef = spread_out(few_lam, spread_lam) * spread_out(few_sig, spread_sig)
    pair_coef = pair_coef.astype(jnp.bfloat16)
    low = lax.broadcasted_iota(jnp.int32, (16, 128), 1) < SH
    for n in range(4):
        copies[n].wait()
        for part in range(2):
            first = n * 1024 + part * 512
            result = lax.dot_general(
                pair_coef, ints[first:first + 512, :], (((1,), (1,)), ((), ())),
                preferred_element_type=jnp.float32,
            )
            for t in range(4):
                mu = first // SH + 2 * t
                for ip in range(2):
                    even = result[ip * 32:ip * 32 + 16, t * 128:t * 128 + 128]
                    odd = result[ip * 32 + 16:ip * 32 + 32, t * 128:t * 128 + 128]
                    lanes = slice(ip * 128, ip * 128 + 128)
                    wide[ip, pl.ds(mu, 16, stride=SH), :] = jnp.where(low, even, pltpu.roll(odd, SH, 1))
                    wide[ip, pl.ds(mu + 1, 16, stride=SH), :] = jnp.where(low, pltpu.roll(even, SH, 1), odd)
    for ip in range(2):
        out_ref[:, ip * 128:ip * 128 + 128] = wide[ip].astype(jnp.bfloat16)


def ket_transform(pair_ints, occ_lam, occ_sig, slabs):
    out = pl.pallas_call(
        ket_kernel,
        out_shape=jax.ShapeDtypeStruct((NJ * 2 * SH, NI * SH), jnp.bfloat16),
        in_specs=[
            pl.BlockSpec(memory_space=pltpu.SMEM),
            pl.BlockSpec(memory_space=pltpu.VMEM),
            pl.BlockSpec(memory_space=pltpu.VMEM),
            pl.BlockSpec(memory_space=pltpu.HBM),
        ],
        out_specs=pl.BlockSpec(memory_space=pltpu.VMEM),
        scratch_shapes=[
            pltpu.VMEM((SH * SH, KL * KS), jnp.bfloat16),
            pltpu.VMEM((2, NJ * 2 * SH, 128), jnp.float32),
            pltpu.SemaphoreType.DMA((4,)),
        ],
        compiler_params=pltpu.CompilerParams(vmem_limit_bytes=VMEM_LIMIT),
        cost_estimate=pl.CostEstimate(flops=140_000_000, bytes_accessed=3_000_000, transcendentals=0),
        name="ket_transform",
    )(slabs, occ_lam, occ_sig.T, pair_ints)
    return out.reshape(NJ, 2, SH, NI * SH)


def ring_place(offset):
    return jnp.where(offset == 0, 0, jnp.where(offset == 3, 1, offset + 1))


def ring_offset(place):
    return jnp.where(place == 0, 0, jnp.where(place == 3, 2, (place * 2 + 1) & 3))


def plan_kernel(place_ref, pairs_ref, across_ref, plan_ref):
    x = place_ref[0]
    y = place_ref[1]
    core = place_ref[3]
    size = (NBLK, NBLK)
    row = lax.broadcasted_iota(jnp.int32, size, 0)
    lane = lax.broadcasted_iota(jnp.int32, size, 1)
    p = row[:, 0:1]
    away_x = (((p >> 2) & 3) - x) & 3
    away_y = ((p & 3) - y) & 3
    inner = ring_place(jnp.where(core == 0, away_x, away_y))
    outer = ring_place(jnp.where(core == 0, away_y, away_x))
    slot = (outer * 4 + inner) * 8 + (p >> 4)
    wide = lax.broadcasted_iota(jnp.int32, (NBLK, 2 * NBLK), 1)

    def total(mask, value, axis):
        picked = jnp.where(mask, value.astype(jnp.float32), 0.0)
        return jnp.sum(picked, axis=axis, keepdims=True).astype(jnp.int32)

    one_down = pairs_ref[:, 0:1]
    two_down = pairs_ref[:, 1:2]
    one_across = across_ref[0:1, :]
    two_across = across_ref[1:2, :]
    lines = []
    targets = []
    for kind in range(2):
        if kind == 0:
            down, across, other = two_down, two_across, one_down
        else:
            other = two_down
            down = jnp.where(one_down == two_down, NBLK - 1, one_down)
            across = jnp.where(one_across == two_across, NBLK - 1, one_across)
        ones = jnp.ones(size, jnp.int32)
        rank = total((down == across) & (lane < row), ones, 1)
        groups_across = jnp.where(lane[0:1] < NSH, (total(down == lane, ones, 0) + 3) >> 2, 0)
        groups_down = jnp.where(row[:, 0:1] < NSH, (total(across == row, ones, 1) + 3) >> 2, 0)
        groups_square = jnp.broadcast_to(groups_across, size)
        before_term = total(lane < down, groups_square, 1)
        before_shell = total(lane < row, groups_square, 1)
        position = jnp.where(down < NSH, before_term * 4 + rank, -1)
        entry = jnp.broadcast_to(other * 256 + slot - NBLK, wide.shape)
        lines.append(total(position == wide, entry, 0) + NBLK)
        here = (lane >= before_shell) & (lane < before_shell + groups_down)
        shell = total(here, row - NSH, 0) + NSH
        number = jnp.sum(groups_across.astype(jnp.float32), axis=1, keepdims=True).astype(jnp.int32)
        targets.append(jnp.concatenate([shell, jnp.broadcast_to(number, shell.shape)], axis=1))
    plan_ref[...] = jnp.concatenate(lines + targets + lines + targets, axis=0)


def plan_terms(shell_pairs, place):
    return pl.pallas_call(
        plan_kernel,
        out_shape=jax.ShapeDtypeStruct((8, 2 * NBLK), jnp.int32),
        in_specs=[
            pl.BlockSpec(memory_space=pltpu.SMEM),
            pl.BlockSpec(memory_space=pltpu.VMEM),
            pl.BlockSpec(memory_space=pltpu.VMEM),
        ],
        out_specs=pl.BlockSpec(memory_space=pltpu.VMEM),
        compiler_params=pltpu.CompilerParams(vmem_limit_bytes=VMEM_LIMIT),
        cost_estimate=pl.CostEstimate(flops=2_000_000, bytes_accessed=10_000, transcendentals=0),
        name="plan_terms",
    )(place, shell_pairs, shell_pairs.T)


UNROLL = 8
FIRSTS = (0, 32, 64, 96, 112, 128)


def build_left(plan_ref, halves, panel_hbm, left, scratch, start_others=lambda: None):
    blocks, panel, lhs, acc, sem_blocks, sem_panel = scratch
    copy_panel = pltpu.make_async_copy(panel_hbm, panel, sem_panel)
    copy_panel.start()
    copies = [
        pltpu.make_async_copy(
            halves[i], blocks.at[pl.ds(FIRSTS[i], FIRSTS[i + 1] - FIRSTS[i])], sem_blocks.at[i]
        )
        for i in range(5)
    ]
    for copy in copies:
        copy.start()
    others = start_others()
    blocks[NBLK] = jnp.zeros(blocks.shape[1:], jnp.bfloat16)

    @pl.loop(0, NSH)
    def _(shell):
        acc[shell] = jnp.zeros(acc.shape[1:], jnp.float32)

    copy_panel.wait()
    for shell in range(NSH):
        rows = panel[shell * SH:(shell + 1) * SH, :]
        lhs[shell] = jnp.concatenate([rows, rows], axis=0).T
    low = lax.broadcasted_iota(jnp.int32, (PANEL, 128), 1) < SH
    low_rows = lax.broadcasted_iota(jnp.int32, (SH, 128), 1) < SH
    for copy in copies:
        copy.wait()

    def terms(kind, group):
        entries = [plan_ref[kind, group * 4 + k] for k in range(4)]
        target = plan_ref[2 + kind, group]
        factor = jnp.concatenate(
            [
                jnp.where(low, lhs[entries[2 * h] >> 8], lhs[entries[2 * h + 1] >> 8])
                for h in range(2)
            ],
            axis=1,
        )
        values = [blocks[entry & 255] for entry in entries]
        if kind == 0:
            return target, jnp.dot(
                factor, jnp.concatenate(values, axis=0), preferred_element_type=jnp.float32
            )
        columns = []
        for h in range(2):
            stack = []
            for rp in range(2):
                a = values[2 * h][:, rp * 128:rp * 128 + 128]
                b = values[2 * h + 1][:, rp * 128:rp * 128 + 128]
                stack.append(jnp.where(low_rows, a, pltpu.roll(b, SH, 1)))
                stack.append(jnp.where(low_rows, pltpu.roll(a, SH, 1), b))
            columns.append(jnp.concatenate(stack, axis=0))
        return target, lax.dot_general(
            factor, jnp.concatenate(columns, axis=1), (((1,), (1,)), ((), ())),
            preferred_element_type=jnp.float32,
        )

    for kind in range(2):
        steps = (plan_ref[2 + kind, NBLK] + UNROLL - 1) // UNROLL

        @pl.loop(0, steps)
        def _(step):
            for u in range(UNROLL):
                target, sums = terms(kind, step * UNROLL + u)
                acc[target] += sums

    @pl.loop(0, NSH // 2)
    def _(t):
        for rp in range(2):
            even = acc[2 * t, :, rp * 128:rp * 128 + 128]
            odd = acc[2 * t + 1, :, rp * 128:rp * 128 + 128]
            columns = pl.ds(pl.multiple_of(t * 128, 128), 128)
            left[rp * 2 * PANEL:(rp * 2 + 1) * PANEL, columns] = jnp.where(
                low, even, pltpu.roll(odd, SH, 1)
            ).astype(jnp.bfloat16)
            left[(rp * 2 + 1) * PANEL:(rp * 2 + 2) * PANEL, columns] = jnp.where(
                low, pltpu.roll(even, SH, 1), odd
            ).astype(jnp.bfloat16)
    return others


LEFT_SCRATCH = [
    pltpu.VMEM((NBLK + 1, SH, NI * SH), jnp.bfloat16),
    pltpu.VMEM((NAO, PANEL), jnp.bfloat16),
    pltpu.VMEM((NSH, PANEL, 2 * SH), jnp.bfloat16),
    pltpu.VMEM((NSH + 1, PANEL, NI * SH), jnp.float32),
    pltpu.SemaphoreType.DMA((5,)),
    pltpu.SemaphoreType.DMA,
]


def start_coefs(place_ref, pieces, coefs, sems):
    z = place_ref[2]
    core = place_ref[3]
    copies = []
    for k in range(10):
        offset = (0, 3, 1, 2, 2)[k % 5]
        base, slots = ((0, 16), (0, 16), (0, 16), (0, 8), (8, 8))[k % 5]
        chunk = ((z + offset) & 3) * 2 + (core if k < 5 else 1 - core)
        copies.append(
            pltpu.make_async_copy(pieces[k], coefs.at[chunk, pl.ds(base, slots)], sems.at[k])
        )
    for copy in copies:
        copy.start()
    return copies


def multiply(place_ref, left, coefs, out_ref, staged, sem_out):
    x = place_ref[0]
    y = place_ref[1]

    def slot_of(panel, which_core):
        there = (panel >> 2, panel & 3)
        first = (there[0] - x) & 3
        second = (there[1] - y) & 3
        if which_core == 1:
            first, second = second, first
        return ring_place(second) * 4 + ring_place(first)

    def out_copy(n, slot):
        return pltpu.make_async_copy(
            staged.at[slot],
            out_ref.at[:, :, pl.ds(pl.multiple_of(n * 256, 256), 256)],
            sem_out.at[slot],
        )

    @pl.loop(0, ACT // 256)
    def _(n):
        slot = n % 2

        @pl.when(n >= 2)
        def _():
            out_copy(n - 2, slot).wait()

        slots = [[slot_of(2 * n + h, c) for h in range(2)] for c in range(2)]
        rhs = jnp.concatenate(
            [
                jnp.concatenate([coefs[chunk, slots[chunk % 2][h]] for h in range(2)], axis=1)
                for chunk in range(8)
            ],
            axis=0,
        )
        for slab in range(2):
            product = jnp.dot(left[slab], rhs, preferred_element_type=jnp.float32)
            staged[slot, slab] = product.astype(jnp.bfloat16)
        out_copy(n, slot).start()

    out_copy(ACT // 256 - 2, 0).wait()
    out_copy(ACT // 256 - 1, 1).wait()


def left_kernel(*refs):
    build_left(refs[0], refs[1:6], refs[6], refs[7], refs[8:])


def left_of_slab(plan, halves, panel):
    return pl.pallas_call(
        left_kernel,
        out_shape=jax.ShapeDtypeStruct((ROWS, NAO), jnp.bfloat16),
        in_specs=[pl.BlockSpec(memory_space=pltpu.SMEM)] + [pl.BlockSpec(memory_space=pltpu.HBM)] * 6,
        out_specs=pl.BlockSpec(memory_space=pltpu.VMEM),
        scratch_shapes=LEFT_SCRATCH,
        compiler_params=pltpu.CompilerParams(vmem_limit_bytes=VMEM_LIMIT),
        cost_estimate=pl.CostEstimate(flops=9_000_000_000, bytes_accessed=7_000_000, transcendentals=0),
        name="left_of_slab",
    )(plan, *halves, panel)


def finish_kernel(*refs):
    plan_ref, place_ref = refs[:2]
    out_ref, coefs, left, staged, sem_coefs, sem_out, sem_left = refs[19:26]

    def start_others():
        copy_left = pltpu.make_async_copy(refs[18], left.at[0], sem_left)
        copy_left.start()
        return [copy_left] + start_coefs(place_ref, refs[8:18], coefs, sem_coefs)

    copies = build_left(plan_ref, refs[2:7], refs[7], left.at[1], refs[26:], start_others)
    for copy in copies:
        copy.wait()
    multiply(place_ref, left, coefs, out_ref, staged, sem_out)


def finish(plan, place, halves, panel, pieces, left):
    return pl.pallas_call(
        finish_kernel,
        out_shape=jax.ShapeDtypeStruct((2, ROWS, ACT), jnp.bfloat16),
        in_specs=[pl.BlockSpec(memory_space=pltpu.SMEM)] * 2 + [pl.BlockSpec(memory_space=pltpu.HBM)] * 17,
        out_specs=pl.BlockSpec(memory_space=pltpu.HBM),
        scratch_shapes=[
            pltpu.VMEM((8, 16, 256, PANEL), jnp.bfloat16),
            pltpu.VMEM((2, ROWS, NAO), jnp.bfloat16),
            pltpu.VMEM((2, 2, ROWS, 256), jnp.bfloat16),
            pltpu.SemaphoreType.DMA((10,)),
            pltpu.SemaphoreType.DMA((2,)),
            pltpu.SemaphoreType.DMA,
        ] + LEFT_SCRATCH,
        compiler_params=pltpu.CompilerParams(vmem_limit_bytes=VMEM_LIMIT),
        cost_estimate=pl.CostEstimate(flops=18_000_000_000, bytes_accessed=20_000_000, transcendentals=0),
        name="finish",
    )(plan, place, *halves, panel, *pieces, left)


def body(pair_ints, shell_pairs, occ_lam, occ_sig, coef_act, slabs):
    ao_index = lax.axis_index("ao")
    mo_index = lax.axis_index("mo")
    place = jnp.stack([mo_index >> 2, mo_index & 3, ao_index >> 1, ao_index & 1]).astype(jnp.int32)

    up, down = plane_pairs(1, 1), plane_pairs(-1, 1)
    z_up, z_down = z_pairs(1), z_pairs(-1)
    swap = device_pairs(lambda x, y, z, c: (x, y, z, 1 - c))

    half = ket_transform(pair_ints, occ_lam, occ_sig, slabs)
    owned = lax.all_to_all(half, "ao", split_axis=0, concat_axis=0, tiled=True)
    chunk = lax.dynamic_slice_in_dim(after(coef_act, half), ao_index * 256, 256, 0)
    with jax.named_scope("s_c1"):
        row = jnp.stack(direct(chunk, 0))
    with jax.named_scope("s_c2"):
        whole = jnp.concatenate(direct(row, 1), axis=0)
    with jax.named_scope("s_p1"):
        near = direct(owned, 0)
        near_first, near_second = [
            jnp.concatenate([piece[:, k] for piece in near], axis=0) for k in range(2)
        ]
    with jax.named_scope("s_p2a"):
        first = both_ways(near_first, up, down)
    plan = plan_terms(after(shell_pairs, half), place)
    with jax.named_scope("s_z1"):
        column = both_ways(after(whole, near_first, plan), z_up, z_down)
    with jax.named_scope("s_p2b"):
        second = both_ways(after(near_second, *first), up, down)
    with jax.named_scope("s_f2a"):
        first += far_halves(first, up, down)
    with jax.named_scope("s_zf"):
        column += far_halves(column, z_up, z_down, *first[3:])
    left = left_of_slab(plan, first, coef_act)
    with jax.named_scope("s_f2b"):
        second += far_halves(second, up, down, left)
    with jax.named_scope("s_swap"):
        pieces = list(column) + [send(after(piece, first[4]), swap) for piece in column]
    out = finish(plan, place, second, coef_act, pieces, left)
    return out.reshape(2, 1, NI, PANEL, ACT)


def solution(mesh):
    return jax.shard_map(
        body,
        mesh=mesh,
        in_specs=(P(("ao", "mo"), None, None), P(), P(), P(), P(None, "mo"), P()),
        out_specs=P(None, "ao", None, "mo", None),
        check_vma=False,
    )
```

```python
import functools

import jax
import jax.numpy as jnp
from jax import lax
from jax.experimental import pallas as pl
from jax.experimental.pallas import tpu as pltpu
from jax.sharding import PartitionSpec as P

SH = 64
NSH = 32
NAO = 2048
ACT = 2048
KL = 16
KS = 16
NI = 4
NJ = 8
NOCC = 32
NBLK = 128
PANEL = 128
ROWS = NI * PANEL
VMEM_LIMIT = 60 << 20
AXES = ("ao", "mo")


def device_pairs(move):
    pairs = []
    for z in range(4):
        for c in range(2):
            for x in range(4):
                for y in range(4):
                    x2, y2, z2, c2 = move(x, y, z, c)
                    source = (z * 2 + c) * 16 + x * 4 + y
                    target = ((z2 % 4) * 2 + c2) * 16 + (x2 % 4) * 4 + y2 % 4
                    pairs.append((source, target))
    return pairs


def plane_pairs(step, phase):
    return device_pairs(
        lambda x, y, z, c: (x + step, y, z, c) if c == phase else (x, y + step, z, c)
    )


def z_pairs(step):
    return device_pairs(lambda x, y, z, c: (x, y, z + step, c))


def send(value, pairs):
    return lax.ppermute(value, AXES, pairs)


def after(value, *others):
    return lax.optimization_barrier((value, *others))[0]


def both_ways(value, pairs_up, pairs_down):
    return value, send(value, pairs_up), send(value, pairs_down)


def far_halves(pieces, pairs_up, pairs_down, *others):
    half = pieces[0].shape[0] // 2
    return (
        send(after(pieces[1], *others)[:half], pairs_up),
        send(after(pieces[2], *others)[half:], pairs_down),
    )


def direct(value, phase):
    return [value] + [send(value, plane_pairs(step, phase)) for step in (1, -1, 2)]


def ket_kernel(slabs_ref, lam_ref, sig_ref, ints_hbm, out_ref, ints, wide, sems):
    copies = [
        pltpu.make_async_copy(
            ints_hbm.at[0, pl.ds(n * 1024, 1024)], ints.at[pl.ds(n * 1024, 1024)], sems.at[n]
        )
        for n in range(4)
    ]
    for copy in copies:
        copy.start()
    rows = lax.broadcasted_iota(jnp.int32, (64, NOCC), 0)
    column = lax.broadcasted_iota(jnp.int32, (64, NOCC), 1)
    number = jnp.where((rows & 1) == 0, slabs_ref[0], slabs_ref[1]) * NI + (rows >> 4)
    pick_lam = jnp.where(column == number, 1.0, 0.0).astype(jnp.bfloat16)
    rows = lax.broadcasted_iota(jnp.int32, (64, NJ), 0)
    column = lax.broadcasted_iota(jnp.int32, (64, NJ), 1)
    pick_sig = jnp.where(column == ((rows >> 1) & 7), 1.0, 0.0).astype(jnp.bfloat16)
    line = lax.broadcasted_iota(jnp.int32, (KL, KL * KS), 0)
    word = lax.broadcasted_iota(jnp.int32, (KL, KL * KS), 1)
    spread_lam = jnp.where((word >> 4) == line, 1.0, 0.0).astype(jnp.bfloat16)
    spread_sig = jnp.where((word & 15) == line, 1.0, 0.0).astype(jnp.bfloat16)

    few_lam = lax.dot_general(
        pick_lam, lam_ref[...], (((1,), (1,)), ((), ())), preferred_element_type=jnp.float32
    )
    few_sig = jnp.dot(pick_sig, sig_ref[...], preferred_element_type=jnp.float32)

    def spread_out(few, spread):
        return jnp.dot(few.astype(jnp.bfloat16), spread, preferred_element_type=jnp.float32)

    pair_coef = spread_out(few_lam, spread_lam) * spread_out(few_sig, spread_sig)
    pair_coef = pair_coef.astype(jnp.bfloat16)
    low = lax.broadcasted_iota(jnp.int32, (16, 128), 1) < SH
    for n in range(4):
        copies[n].wait()
        for part in range(2):
            first = n * 1024 + part * 512
            result = lax.dot_general(
                pair_coef, ints[first:first + 512, :], (((1,), (1,)), ((), ())),
                preferred_element_type=jnp.float32,
            )
            for t in range(4):
                mu = first // SH + 2 * t
                for ip in range(2):
                    even = result[ip * 32:ip * 32 + 16, t * 128:t * 128 + 128]
                    odd = result[ip * 32 + 16:ip * 32 + 32, t * 128:t * 128 + 128]
                    lanes = slice(ip * 128, ip * 128 + 128)
                    wide[ip, pl.ds(mu, 16, stride=SH), :] = jnp.where(low, even, pltpu.roll(odd, SH, 1))
                    wide[ip, pl.ds(mu + 1, 16, stride=SH), :] = jnp.where(low, pltpu.roll(even, SH, 1), odd)
    for ip in range(2):
        out_ref[:, ip * 128:ip * 128 + 128] = wide[ip].astype(jnp.bfloat16)


def ket_transform(pair_ints, occ_lam, occ_sig, slabs):
    out = pl.pallas_call(
        ket_kernel,
        out_shape=jax.ShapeDtypeStruct((NJ * 2 * SH, NI * SH), jnp.bfloat16),
        in_specs=[
            pl.BlockSpec(memory_space=pltpu.SMEM),
            pl.BlockSpec(memory_space=pltpu.VMEM),
            pl.BlockSpec(memory_space=pltpu.VMEM),
            pl.BlockSpec(memory_space=pltpu.HBM),
        ],
        out_specs=pl.BlockSpec(memory_space=pltpu.VMEM),
        scratch_shapes=[
            pltpu.VMEM((SH * SH, KL * KS), jnp.bfloat16),
            pltpu.VMEM((2, NJ * 2 * SH, 128), jnp.float32),
            pltpu.SemaphoreType.DMA((4,)),
        ],
        compiler_params=pltpu.CompilerParams(vmem_limit_bytes=VMEM_LIMIT),
        cost_estimate=pl.CostEstimate(flops=140_000_000, bytes_accessed=3_000_000, transcendentals=0),
        name="ket_transform",
    )(slabs, occ_lam, occ_sig.T, pair_ints)
    return out.reshape(NJ, 2, SH, NI * SH)


def ring_place(offset):
    return jnp.where(offset == 0, 0, jnp.where(offset == 3, 1, offset + 1))


def ring_offset(place):
    return jnp.where(place == 0, 0, jnp.where(place == 3, 2, (place * 2 + 1) & 3))


def plan_kernel(place_ref, pairs_ref, across_ref, plan_ref):
    x = place_ref[0]
    y = place_ref[1]
    core = place_ref[3]
    size = (NBLK, NBLK)
    row = lax.broadcasted_iota(jnp.int32, size, 0)
    lane = lax.broadcasted_iota(jnp.int32, size, 1)
    p = row[:, 0:1]
    away_x = (((p >> 2) & 3) - x) & 3
    away_y = ((p & 3) - y) & 3
    inner = ring_place(jnp.where(core == 0, away_x, away_y))
    outer = ring_place(jnp.where(core == 0, away_y, away_x))
    slot = (outer * 4 + inner) * 8 + (p >> 4)
    wide = lax.broadcasted_iota(jnp.int32, (NBLK, 2 * NBLK), 1)

    def total(mask, value, axis):
        picked = jnp.where(mask, value.astype(jnp.float32), 0.0)
        return jnp.sum(picked, axis=axis, keepdims=True).astype(jnp.int32)

    one_down = pairs_ref[:, 0:1]
    two_down = pairs_ref[:, 1:2]
    one_across = across_ref[0:1, :]
    two_across = across_ref[1:2, :]
    lines = []
    targets = []
    for kind in range(2):
        if kind == 0:
            down, across, other = two_down, two_across, one_down
        else:
            other = two_down
            down = jnp.where(one_down == two_down, NBLK - 1, one_down)
            across = jnp.where(one_across == two_across, NBLK - 1, one_across)
        ones = jnp.ones(size, jnp.int32)
        rank = total((down == across) & (lane < row), ones, 1)
        groups_across = jnp.where(lane[0:1] < NSH, (total(down == lane, ones, 0) + 3) >> 2, 0)
        groups_down = jnp.where(row[:, 0:1] < NSH, (total(across == row, ones, 1) + 3) >> 2, 0)
        groups_square = jnp.broadcast_to(groups_across, size)
        before_term = total(lane < down, groups_square, 1)
        before_shell = total(lane < row, groups_square, 1)
        position = jnp.where(down < NSH, before_term * 4 + rank, -1)
        entry = jnp.broadcast_to(other * 256 + slot - NBLK, wide.shape)
        lines.append(total(position == wide, entry, 0) + NBLK)
        here = (lane >= before_shell) & (lane < before_shell + groups_down)
        shell = total(here, row - NSH, 0) + NSH
        number = jnp.sum(groups_across.astype(jnp.float32), axis=1, keepdims=True).astype(jnp.int32)
        targets.append(jnp.concatenate([shell, jnp.broadcast_to(number, shell.shape)], axis=1))
    plan_ref[...] = jnp.concatenate(lines + targets + lines + targets, axis=0)


def plan_terms(shell_pairs, place):
    return pl.pallas_call(
        plan_kernel,
        out_shape=jax.ShapeDtypeStruct((8, 2 * NBLK), jnp.int32),
        in_specs=[
            pl.BlockSpec(memory_space=pltpu.SMEM),
            pl.BlockSpec(memory_space=pltpu.VMEM),
            pl.BlockSpec(memory_space=pltpu.VMEM),
        ],
        out_specs=pl.BlockSpec(memory_space=pltpu.VMEM),
        compiler_params=pltpu.CompilerParams(vmem_limit_bytes=VMEM_LIMIT),
        cost_estimate=pl.CostEstimate(flops=2_000_000, bytes_accessed=10_000, transcendentals=0),
        name="plan_terms",
    )(place, shell_pairs, shell_pairs.T)


UNROLL = 8
FIRSTS = (0, 32, 64, 96, 112, 128)


def build_left(plan_ref, halves, panel_hbm, left, scratch, start_others=lambda: None):
    blocks, panel, lhs, acc, sem_blocks, sem_panel = scratch
    copy_panel = pltpu.make_async_copy(panel_hbm, panel, sem_panel)
    copy_panel.start()
    copies = [
        pltpu.make_async_copy(
            halves[i], blocks.at[pl.ds(FIRSTS[i], FIRSTS[i + 1] - FIRSTS[i])], sem_blocks.at[i]
        )
        for i in range(5)
    ]
    for copy in copies:
        copy.start()
    others = start_others()
    blocks[NBLK] = jnp.zeros(blocks.shape[1:], jnp.bfloat16)

    @pl.loop(0, NSH)
    def _(shell):
        acc[shell] = jnp.zeros(acc.shape[1:], jnp.float32)

    copy_panel.wait()
    for shell in range(NSH):
        rows = panel[shell * SH:(shell + 1) * SH, :]
        lhs[shell] = jnp.concatenate([rows, rows], axis=0).T
    low = lax.broadcasted_iota(jnp.int32, (PANEL, 128), 1) < SH
    low_rows = lax.broadcasted_iota(jnp.int32, (SH, 128), 1) < SH
    for copy in copies:
        copy.wait()

    def terms(kind, group):
        entries = [plan_ref[kind, group * 4 + k] for k in range(4)]
        target = plan_ref[2 + kind, group]
        factor = jnp.concatenate(
            [
                jnp.where(low, lhs[entries[2 * h] >> 8], lhs[entries[2 * h + 1] >> 8])
                for h in range(2)
            ],
            axis=1,
        )
        values = [blocks[entry & 255] for entry in entries]
        if kind == 0:
            return target, jnp.dot(
                factor, jnp.concatenate(values, axis=0), preferred_element_type=jnp.float32
            )
        columns = []
        for h in range(2):
            stack = []
            for rp in range(2):
                a = values[2 * h][:, rp * 128:rp * 128 + 128]
                b = values[2 * h + 1][:, rp * 128:rp * 128 + 128]
                stack.append(jnp.where(low_rows, a, pltpu.roll(b, SH, 1)))
                stack.append(jnp.where(low_rows, pltpu.roll(a, SH, 1), b))
            columns.append(jnp.concatenate(stack, axis=0))
        return target, lax.dot_general(
            factor, jnp.concatenate(columns, axis=1), (((1,), (1,)), ((), ())),
            preferred_element_type=jnp.float32,
        )

    for kind in range(2):
        steps = (plan_ref[2 + kind, NBLK] + UNROLL - 1) // UNROLL

        @pl.loop(0, steps)
        def _(step):
            for u in range(UNROLL):
                target, sums = terms(kind, step * UNROLL + u)
                acc[target] += sums

    @pl.loop(0, NSH // 2)
    def _(t):
        for rp in range(2):
            even = acc[2 * t, :, rp * 128:rp * 128 + 128]
            odd = acc[2 * t + 1, :, rp * 128:rp * 128 + 128]
            columns = pl.ds(pl.multiple_of(t * 128, 128), 128)
            left[rp * 2 * PANEL:(rp * 2 + 1) * PANEL, columns] = jnp.where(
                low, even, pltpu.roll(odd, SH, 1)
            ).astype(jnp.bfloat16)
            left[(rp * 2 + 1) * PANEL:(rp * 2 + 2) * PANEL, columns] = jnp.where(
                low, pltpu.roll(even, SH, 1), odd
            ).astype(jnp.bfloat16)
    return others


LEFT_SCRATCH = [
    pltpu.VMEM((NBLK + 1, SH, NI * SH), jnp.bfloat16),
    pltpu.VMEM((NAO, PANEL), jnp.bfloat16),
    pltpu.VMEM((NSH, PANEL, 2 * SH), jnp.bfloat16),
    pltpu.VMEM((NSH + 1, PANEL, NI * SH), jnp.float32),
    pltpu.SemaphoreType.DMA((5,)),
    pltpu.SemaphoreType.DMA,
]


def start_coefs(place_ref, pieces, coefs, sems):
    z = place_ref[2]
    core = place_ref[3]
    copies = []
    for k in range(10):
        offset = (0, 3, 1, 2, 2)[k % 5]
        base, slots = ((0, 16), (0, 16), (0, 16), (0, 8), (8, 8))[k % 5]
        chunk = ((z + offset) & 3) * 2 + (core if k < 5 else 1 - core)
        copies.append(
            pltpu.make_async_copy(pieces[k], coefs.at[chunk, pl.ds(base, slots)], sems.at[k])
        )
    for copy in copies:
        copy.start()
    return copies


def multiply(place_ref, left, coefs, out_ref, staged, sem_out):
    x = place_ref[0]
    y = place_ref[1]

    def slot_of(panel, which_core):
        there = (panel >> 2, panel & 3)
        first = (there[0] - x) & 3
        second = (there[1] - y) & 3
        if which_core == 1:
            first, second = second, first
        return ring_place(second) * 4 + ring_place(first)

    def out_copy(n, slot):
        return pltpu.make_async_copy(
            staged.at[slot],
            out_ref.at[:, :, pl.ds(pl.multiple_of(n * 256, 256), 256)],
            sem_out.at[slot],
        )

    @pl.loop(0, ACT // 256)
    def _(n):
        slot = n % 2

        @pl.when(n >= 2)
        def _():
            out_copy(n - 2, slot).wait()

        slots = [[slot_of(2 * n + h, c) for h in range(2)] for c in range(2)]
        rhs = jnp.concatenate(
            [
                jnp.concatenate([coefs[chunk, slots[chunk % 2][h]] for h in range(2)], axis=1)
                for chunk in range(8)
            ],
            axis=0,
        )
        for slab in range(2):
            product = jnp.dot(left[slab], rhs, preferred_element_type=jnp.float32)
            staged[slot, slab] = product.astype(jnp.bfloat16)
        out_copy(n, slot).start()

    out_copy(ACT // 256 - 2, 0).wait()
    out_copy(ACT // 256 - 1, 1).wait()


def left_kernel(*refs):
    build_left(refs[0], refs[1:6], refs[6], refs[7], refs[8:])


def left_of_slab(plan, halves, panel):
    return pl.pallas_call(
        left_kernel,
        out_shape=jax.ShapeDtypeStruct((ROWS, NAO), jnp.bfloat16),
        in_specs=[pl.BlockSpec(memory_space=pltpu.SMEM)] + [pl.BlockSpec(memory_space=pltpu.HBM)] * 6,
        out_specs=pl.BlockSpec(memory_space=pltpu.VMEM),
        scratch_shapes=LEFT_SCRATCH,
        compiler_params=pltpu.CompilerParams(vmem_limit_bytes=16 << 20),
        cost_estimate=pl.CostEstimate(flops=9_000_000_000, bytes_accessed=7_000_000, transcendentals=0),
        name="left_of_slab",
    )(plan, *halves, panel)


def finish_kernel(*refs):
    plan_ref, place_ref = refs[:2]
    out_ref, coefs, left, staged, sem_coefs, sem_out, sem_left = refs[19:26]

    def start_others():
        copy_left = pltpu.make_async_copy(refs[18], left.at[0], sem_left)
        copy_left.start()
        return [copy_left] + start_coefs(place_ref, refs[8:18], coefs, sem_coefs)

    copies = build_left(plan_ref, refs[2:7], refs[7], left.at[1], refs[26:], start_others)
    for copy in copies:
        copy.wait()
    multiply(place_ref, left, coefs, out_ref, staged, sem_out)


def finish(plan, place, halves, panel, pieces, left):
    return pl.pallas_call(
        finish_kernel,
        out_shape=jax.ShapeDtypeStruct((2, ROWS, ACT), jnp.bfloat16),
        in_specs=[pl.BlockSpec(memory_space=pltpu.SMEM)] * 2 + [pl.BlockSpec(memory_space=pltpu.HBM)] * 17,
        out_specs=pl.BlockSpec(memory_space=pltpu.HBM),
        scratch_shapes=[
            pltpu.VMEM((8, 16, 256, PANEL), jnp.bfloat16),
            pltpu.VMEM((2, ROWS, NAO), jnp.bfloat16),
            pltpu.VMEM((2, 2, ROWS, 256), jnp.bfloat16),
            pltpu.SemaphoreType.DMA((10,)),
            pltpu.SemaphoreType.DMA((2,)),
            pltpu.SemaphoreType.DMA,
        ] + LEFT_SCRATCH,
        compiler_params=pltpu.CompilerParams(vmem_limit_bytes=28 << 20),
        cost_estimate=pl.CostEstimate(flops=18_000_000_000, bytes_accessed=20_000_000, transcendentals=0),
        name="finish",
    )(plan, place, *halves, panel, *pieces, left)


def body(pair_ints, shell_pairs, occ_lam, occ_sig, coef_act, slabs):
    ao_index = lax.axis_index("ao")
    mo_index = lax.axis_index("mo")
    place = jnp.stack([mo_index >> 2, mo_index & 3, ao_index >> 1, ao_index & 1]).astype(jnp.int32)

    up, down = plane_pairs(1, 1), plane_pairs(-1, 1)
    z_up, z_down = z_pairs(1), z_pairs(-1)
    swap = device_pairs(lambda x, y, z, c: (x, y, z, 1 - c))

    half = ket_transform(pair_ints, occ_lam, occ_sig, slabs)
    owned = lax.all_to_all(half, "ao", split_axis=0, concat_axis=0, tiled=True)
    chunk = lax.dynamic_slice_in_dim(after(coef_act, half), ao_index * 256, 256, 0)
    with jax.named_scope("s_c1"):
        row = jnp.stack(direct(chunk, 0))
    with jax.named_scope("s_c2"):
        whole = jnp.concatenate(direct(row, 1), axis=0)
    with jax.named_scope("s_p1"):
        near = direct(owned, 0)
        near_first, near_second = [
            jnp.concatenate([piece[:, k] for piece in near], axis=0) for k in range(2)
        ]
    with jax.named_scope("s_p2a"):
        first = both_ways(near_first, up, down)
    plan = plan_terms(after(shell_pairs, half), place)
    with jax.named_scope("s_z1"):
        column = both_ways(after(whole, near_first, plan), z_up, z_down)
    with jax.named_scope("s_p2b"):
        second = both_ways(after(near_second, *first), up, down)
    with jax.named_scope("s_f2a"):
        first += far_halves(first, up, down)
    with jax.named_scope("s_zf"):
        column += far_halves(column, z_up, z_down, *first[3:])
    left = left_of_slab(plan, first, coef_act)
    with jax.named_scope("s_f2b"):
        second += far_halves(second, up, down, left)
    with jax.named_scope("s_swap"):
        pieces = list(column) + [send(after(piece, first[4]), swap) for piece in column]
    out = finish(plan, place, second, coef_act, pieces, left)
    return out.reshape(2, 1, NI, PANEL, ACT)


def solution(mesh):
    return jax.shard_map(
        body,
        mesh=mesh,
        in_specs=(P(("ao", "mo"), None, None), P(), P(), P(), P(None, "mo"), P()),
        out_specs=P(None, "ao", None, "mo", None),
        check_vma=False,
    )
```

```python
import functools

import jax
import jax.numpy as jnp
from jax import lax
from jax.experimental import pallas as pl
from jax.experimental.pallas import tpu as pltpu
from jax.sharding import PartitionSpec as P

SH = 64
NSH = 32
NAO = 2048
ACT = 2048
KL = 16
KS = 16
NI = 4
NJ = 8
NOCC = 32
NBLK = 128
PANEL = 128
ROWS = NI * PANEL
VMEM_LIMIT = 60 << 20
AXES = ("ao", "mo")


def device_pairs(move):
    pairs = []
    for z in range(4):
        for c in range(2):
            for x in range(4):
                for y in range(4):
                    x2, y2, z2, c2 = move(x, y, z, c)
                    source = (z * 2 + c) * 16 + x * 4 + y
                    target = ((z2 % 4) * 2 + c2) * 16 + (x2 % 4) * 4 + y2 % 4
                    pairs.append((source, target))
    return pairs


def plane_pairs(step, phase):
    return device_pairs(
        lambda x, y, z, c: (x + step, y, z, c) if c == phase else (x, y + step, z, c)
    )


def z_pairs(step):
    return device_pairs(lambda x, y, z, c: (x, y, z + step, c))


def send(value, pairs):
    return lax.ppermute(value, AXES, pairs)


def after(value, *others):
    return lax.optimization_barrier((value, *others))[0]


def both_ways(value, pairs_up, pairs_down):
    return value, send(value, pairs_up), send(value, pairs_down)


def far_halves(pieces, pairs_up, pairs_down, *others):
    half = pieces[0].shape[0] // 2
    return (
        send(after(pieces[1], *others)[:half], pairs_up),
        send(after(pieces[2], *others)[half:], pairs_down),
    )


def direct(value, phase):
    return [value] + [send(value, plane_pairs(step, phase)) for step in (1, -1, 2)]


def ket_kernel(slabs_ref, lam_ref, sig_ref, ints_hbm, out_ref, ints, wide, sems):
    copies = [
        pltpu.make_async_copy(
            ints_hbm.at[0, pl.ds(n * 1024, 1024)], ints.at[pl.ds(n * 1024, 1024)], sems.at[n]
        )
        for n in range(4)
    ]
    for copy in copies:
        copy.start()
    rows = lax.broadcasted_iota(jnp.int32, (64, NOCC), 0)
    column = lax.broadcasted_iota(jnp.int32, (64, NOCC), 1)
    number = jnp.where((rows & 1) == 0, slabs_ref[0], slabs_ref[1]) * NI + (rows >> 4)
    pick_lam = jnp.where(column == number, 1.0, 0.0).astype(jnp.bfloat16)
    rows = lax.broadcasted_iota(jnp.int32, (64, NJ), 0)
    column = lax.broadcasted_iota(jnp.int32, (64, NJ), 1)
    pick_sig = jnp.where(column == ((rows >> 1) & 7), 1.0, 0.0).astype(jnp.bfloat16)
    line = lax.broadcasted_iota(jnp.int32, (KL, KL * KS), 0)
    word = lax.broadcasted_iota(jnp.int32, (KL, KL * KS), 1)
    spread_lam = jnp.where((word >> 4) == line, 1.0, 0.0).astype(jnp.bfloat16)
    spread_sig = jnp.where((word & 15) == line, 1.0, 0.0).astype(jnp.bfloat16)

    few_lam = lax.dot_general(
        pick_lam, lam_ref[...], (((1,), (1,)), ((), ())), preferred_element_type=jnp.float32
    )
    few_sig = jnp.dot(pick_sig, sig_ref[...], preferred_element_type=jnp.float32)

    def spread_out(few, spread):
        return jnp.dot(few.astype(jnp.bfloat16), spread, preferred_element_type=jnp.float32)

    pair_coef = spread_out(few_lam, spread_lam) * spread_out(few_sig, spread_sig)
    pair_coef = pair_coef.astype(jnp.bfloat16)
    low = lax.broadcasted_iota(jnp.int32, (16, 128), 1) < SH
    for n in range(4):
        copies[n].wait()
        for part in range(2):
            first = n * 1024 + part * 512
            result = lax.dot_general(
                pair_coef, ints[first:first + 512, :], (((1,), (1,)), ((), ())),
                preferred_element_type=jnp.float32,
            )
            for t in range(4):
                mu = first // SH + 2 * t
                for ip in range(2):
                    even = result[ip * 32:ip * 32 + 16, t * 128:t * 128 + 128]
                    odd = result[ip * 32 + 16:ip * 32 + 32, t * 128:t * 128 + 128]
                    lanes = slice(ip * 128, ip * 128 + 128)
                    wide[ip, pl.ds(mu, 16, stride=SH), :] = jnp.where(low, even, pltpu.roll(odd, SH, 1))
                    wide[ip, pl.ds(mu + 1, 16, stride=SH), :] = jnp.where(low, pltpu.roll(even, SH, 1), odd)
    for ip in range(2):
        out_ref[:, ip * 128:ip * 128 + 128] = wide[ip].astype(jnp.bfloat16)


def ket_transform(pair_ints, occ_lam, occ_sig, slabs):
    out = pl.pallas_call(
        ket_kernel,
        out_shape=jax.ShapeDtypeStruct((NJ * 2 * SH, NI * SH), jnp.bfloat16),
        in_specs=[
            pl.BlockSpec(memory_space=pltpu.SMEM),
            pl.BlockSpec(memory_space=pltpu.VMEM),
            pl.BlockSpec(memory_space=pltpu.VMEM),
            pl.BlockSpec(memory_space=pltpu.HBM),
        ],
        out_specs=pl.BlockSpec(memory_space=pltpu.VMEM),
        scratch_shapes=[
            pltpu.VMEM((SH * SH, KL * KS), jnp.bfloat16),
            pltpu.VMEM((2, NJ * 2 * SH, 128), jnp.float32),
            pltpu.SemaphoreType.DMA((4,)),
        ],
        compiler_params=pltpu.CompilerParams(vmem_limit_bytes=VMEM_LIMIT),
        cost_estimate=pl.CostEstimate(flops=140_000_000, bytes_accessed=3_000_000, transcendentals=0),
        name="ket_transform",
    )(slabs, occ_lam, occ_sig.T, pair_ints)
    return out.reshape(NJ, 2, SH, NI * SH)


def ring_place(offset):
    return jnp.where(offset == 0, 0, jnp.where(offset == 3, 1, offset + 1))


def ring_offset(place):
    return jnp.where(place == 0, 0, jnp.where(place == 3, 2, (place * 2 + 1) & 3))


def plan_kernel(place_ref, pairs_ref, across_ref, plan_ref):
    x = place_ref[0]
    y = place_ref[1]
    core = place_ref[3]
    size = (NBLK, NBLK)
    row = lax.broadcasted_iota(jnp.int32, size, 0)
    lane = lax.broadcasted_iota(jnp.int32, size, 1)
    p = row[:, 0:1]
    away_x = (((p >> 2) & 3) - x) & 3
    away_y = ((p & 3) - y) & 3
    inner = ring_place(jnp.where(core == 0, away_x, away_y))
    outer = ring_place(jnp.where(core == 0, away_y, away_x))
    slot = (outer * 4 + inner) * 8 + (p >> 4)
    wide = lax.broadcasted_iota(jnp.int32, (NBLK, 2 * NBLK), 1)

    def total(mask, value, axis):
        picked = jnp.where(mask, value.astype(jnp.float32), 0.0)
        return jnp.sum(picked, axis=axis, keepdims=True).astype(jnp.int32)

    one_down = pairs_ref[:, 0:1]
    two_down = pairs_ref[:, 1:2]
    one_across = across_ref[0:1, :]
    two_across = across_ref[1:2, :]
    lines = []
    targets = []
    for kind in range(2):
        if kind == 0:
            down, across, other = two_down, two_across, one_down
        else:
            other = two_down
            down = jnp.where(one_down == two_down, NBLK - 1, one_down)
            across = jnp.where(one_across == two_across, NBLK - 1, one_across)
        ones = jnp.ones(size, jnp.int32)
        rank = total((down == across) & (lane < row), ones, 1)
        groups_across = jnp.where(lane[0:1] < NSH, (total(down == lane, ones, 0) + 3) >> 2, 0)
        groups_down = jnp.where(row[:, 0:1] < NSH, (total(across == row, ones, 1) + 3) >> 2, 0)
        groups_square = jnp.broadcast_to(groups_across, size)
        before_term = total(lane < down, groups_square, 1)
        before_shell = total(lane < row, groups_square, 1)
        position = jnp.where(down < NSH, before_term * 4 + rank, -1)
        entry = jnp.broadcast_to(other * 256 + slot - NBLK, wide.shape)
        lines.append(total(position == wide, entry, 0) + NBLK)
        here = (lane >= before_shell) & (lane < before_shell + groups_down)
        shell = total(here, row - NSH, 0) + NSH
        number = jnp.sum(groups_across.astype(jnp.float32), axis=1, keepdims=True).astype(jnp.int32)
        targets.append(jnp.concatenate([shell, jnp.broadcast_to(number, shell.shape)], axis=1))
    plan_ref[...] = jnp.concatenate(lines + targets + lines + targets, axis=0)


def plan_terms(shell_pairs, place):
    return pl.pallas_call(
        plan_kernel,
        out_shape=jax.ShapeDtypeStruct((8, 2 * NBLK), jnp.int32),
        in_specs=[
            pl.BlockSpec(memory_space=pltpu.SMEM),
            pl.BlockSpec(memory_space=pltpu.VMEM),
            pl.BlockSpec(memory_space=pltpu.VMEM),
        ],
        out_specs=pl.BlockSpec(memory_space=pltpu.VMEM),
        compiler_params=pltpu.CompilerParams(vmem_limit_bytes=VMEM_LIMIT),
        cost_estimate=pl.CostEstimate(flops=2_000_000, bytes_accessed=10_000, transcendentals=0),
        name="plan_terms",
    )(place, shell_pairs, shell_pairs.T)


UNROLL = 14
FIRSTS = (0, 32, 64, 96, 112, 128)


def build_left(plan_ref, halves, panel_hbm, left, scratch, start_others=lambda: None):
    blocks, panel, lhs, acc, sem_blocks, sem_panel = scratch
    copy_panel = pltpu.make_async_copy(panel_hbm, panel, sem_panel)
    copy_panel.start()
    copies = [
        pltpu.make_async_copy(
            halves[i], blocks.at[pl.ds(FIRSTS[i], FIRSTS[i + 1] - FIRSTS[i])], sem_blocks.at[i]
        )
        for i in range(5)
    ]
    for copy in copies:
        copy.start()
    others = start_others()
    blocks[NBLK] = jnp.zeros(blocks.shape[1:], jnp.bfloat16)

    @pl.loop(0, NSH)
    def _(shell):
        acc[shell] = jnp.zeros(acc.shape[1:], jnp.float32)

    copy_panel.wait()
    for shell in range(NSH):
        rows = panel[shell * SH:(shell + 1) * SH, :]
        lhs[shell] = jnp.concatenate([rows, rows], axis=0).T
    low = lax.broadcasted_iota(jnp.int32, (PANEL, 128), 1) < SH
    low_rows = lax.broadcasted_iota(jnp.int32, (SH, 128), 1) < SH
    for copy in copies:
        copy.wait()

    def terms(kind, group):
        entries = [plan_ref[kind, group * 4 + k] for k in range(4)]
        target = plan_ref[2 + kind, group]
        factor = jnp.concatenate(
            [
                jnp.where(low, lhs[entries[2 * h] >> 8], lhs[entries[2 * h + 1] >> 8])
                for h in range(2)
            ],
            axis=1,
        )
        values = [blocks[entry & 255] for entry in entries]
        if kind == 0:
            return target, jnp.dot(
                factor, jnp.concatenate(values, axis=0), preferred_element_type=jnp.float32
            )
        columns = []
        for h in range(2):
            stack = []
            for rp in range(2):
                a = values[2 * h][:, rp * 128:rp * 128 + 128]
                b = values[2 * h + 1][:, rp * 128:rp * 128 + 128]
                stack.append(jnp.where(low_rows, a, pltpu.roll(b, SH, 1)))
                stack.append(jnp.where(low_rows, pltpu.roll(a, SH, 1), b))
            columns.append(jnp.concatenate(stack, axis=0))
        return target, lax.dot_general(
            factor, jnp.concatenate(columns, axis=1), (((1,), (1,)), ((), ())),
            preferred_element_type=jnp.float32,
        )

    most = jnp.maximum(plan_ref[2, NBLK], plan_ref[3, NBLK])

    @pl.loop(0, (most + UNROLL - 1) // UNROLL)
    def _(step):
        for u in range(UNROLL):
            for kind in range(2):
                target, sums = terms(kind, step * UNROLL + u)
                acc[target] += sums

    @pl.loop(0, NSH // 2, unroll=4)
    def _(t):
        for rp in range(2):
            even = acc[2 * t, :, rp * 128:rp * 128 + 128]
            odd = acc[2 * t + 1, :, rp * 128:rp * 128 + 128]
            columns = pl.ds(pl.multiple_of(t * 128, 128), 128)
            left[rp * 2 * PANEL:(rp * 2 + 1) * PANEL, columns] = jnp.where(
                low, even, pltpu.roll(odd, SH, 1)
            ).astype(jnp.bfloat16)
            left[(rp * 2 + 1) * PANEL:(rp * 2 + 2) * PANEL, columns] = jnp.where(
                low, pltpu.roll(even, SH, 1), odd
            ).astype(jnp.bfloat16)
    return others


LEFT_SCRATCH = [
    pltpu.VMEM((NBLK + 1, SH, NI * SH), jnp.bfloat16),
    pltpu.VMEM((NAO, PANEL), jnp.bfloat16),
    pltpu.VMEM((NSH, PANEL, 2 * SH), jnp.bfloat16),
    pltpu.VMEM((NSH + 1, PANEL, NI * SH), jnp.float32),
    pltpu.SemaphoreType.DMA((5,)),
    pltpu.SemaphoreType.DMA,
]


def start_coefs(place_ref, pieces, coefs, sems):
    z = place_ref[2]
    core = place_ref[3]
    copies = []
    for k in range(10):
        offset = (0, 3, 1, 2, 2)[k % 5]
        base, slots = ((0, 16), (0, 16), (0, 16), (0, 8), (8, 8))[k % 5]
        chunk = ((z + offset) & 3) * 2 + (core if k < 5 else 1 - core)
        copies.append(
            pltpu.make_async_copy(pieces[k], coefs.at[chunk, pl.ds(base, slots)], sems.at[k])
        )
    for copy in copies:
        copy.start()
    return copies


def multiply(place_ref, left, coefs, out_ref, staged, sem_out):
    x = place_ref[0]
    y = place_ref[1]

    def slot_of(panel, which_core):
        there = (panel >> 2, panel & 3)
        first = (there[0] - x) & 3
        second = (there[1] - y) & 3
        if which_core == 1:
            first, second = second, first
        return ring_place(second) * 4 + ring_place(first)

    def out_copy(n, slot):
        return pltpu.make_async_copy(
            staged.at[slot],
            out_ref.at[:, :, pl.ds(pl.multiple_of(n * 256, 256), 256)],
            sem_out.at[slot],
        )

    @pl.loop(0, ACT // 256, unroll=2)
    def _(n):
        slot = n % 2

        @pl.when(n >= 2)
        def _():
            out_copy(n - 2, slot).wait()

        slots = [[slot_of(2 * n + h, c) for h in range(2)] for c in range(2)]
        rhs = jnp.concatenate(
            [
                jnp.concatenate([coefs[chunk, slots[chunk % 2][h]] for h in range(2)], axis=1)
                for chunk in range(8)
            ],
            axis=0,
        )
        for slab in range(2):
            product = jnp.dot(left[slab], rhs, preferred_element_type=jnp.float32)
            staged[slot, slab] = product.astype(jnp.bfloat16)
        out_copy(n, slot).start()

    out_copy(ACT // 256 - 2, 0).wait()
    out_copy(ACT // 256 - 1, 1).wait()


def left_kernel(*refs):
    build_left(refs[0], refs[1:6], refs[6], refs[7], refs[8:])


def left_of_slab(plan, halves, panel):
    return pl.pallas_call(
        left_kernel,
        out_shape=jax.ShapeDtypeStruct((ROWS, NAO), jnp.bfloat16),
        in_specs=[pl.BlockSpec(memory_space=pltpu.SMEM)] + [pl.BlockSpec(memory_space=pltpu.HBM)] * 6,
        out_specs=pl.BlockSpec(memory_space=pltpu.VMEM),
        scratch_shapes=LEFT_SCRATCH,
        compiler_params=pltpu.CompilerParams(vmem_limit_bytes=16 << 20),
        cost_estimate=pl.CostEstimate(flops=9_000_000_000, bytes_accessed=7_000_000, transcendentals=0),
        name="left_of_slab",
    )(plan, *halves, panel)


def finish_kernel(*refs):
    plan_ref, place_ref = refs[:2]
    out_ref, coefs, left, staged, sem_coefs, sem_out, sem_left = refs[19:26]

    def start_others():
        copy_left = pltpu.make_async_copy(refs[18], left.at[0], sem_left)
        copy_left.start()
        return [copy_left] + start_coefs(place_ref, refs[8:18], coefs, sem_coefs)

    copies = build_left(plan_ref, refs[2:7], refs[7], left.at[1], refs[26:], start_others)
    for copy in copies:
        copy.wait()
    multiply(place_ref, left, coefs, out_ref, staged, sem_out)


def finish(plan, place, halves, panel, pieces, left):
    return pl.pallas_call(
        finish_kernel,
        out_shape=jax.ShapeDtypeStruct((2, ROWS, ACT), jnp.bfloat16),
        in_specs=[pl.BlockSpec(memory_space=pltpu.SMEM)] * 2 + [pl.BlockSpec(memory_space=pltpu.HBM)] * 17,
        out_specs=pl.BlockSpec(memory_space=pltpu.HBM),
        scratch_shapes=[
            pltpu.VMEM((8, 16, 256, PANEL), jnp.bfloat16),
            pltpu.VMEM((2, ROWS, NAO), jnp.bfloat16),
            pltpu.VMEM((2, 2, ROWS, 256), jnp.bfloat16),
            pltpu.SemaphoreType.DMA((10,)),
            pltpu.SemaphoreType.DMA((2,)),
            pltpu.SemaphoreType.DMA,
        ] + LEFT_SCRATCH,
        compiler_params=pltpu.CompilerParams(vmem_limit_bytes=28 << 20),
        cost_estimate=pl.CostEstimate(flops=18_000_000_000, bytes_accessed=20_000_000, transcendentals=0),
        name="finish",
    )(plan, place, *halves, panel, *pieces, left)


def body(pair_ints, shell_pairs, occ_lam, occ_sig, coef_act, slabs):
    ao_index = lax.axis_index("ao")
    mo_index = lax.axis_index("mo")
    place = jnp.stack([mo_index >> 2, mo_index & 3, ao_index >> 1, ao_index & 1]).astype(jnp.int32)

    up, down = plane_pairs(1, 1), plane_pairs(-1, 1)
    z_up, z_down = z_pairs(1), z_pairs(-1)
    swap = device_pairs(lambda x, y, z, c: (x, y, z, 1 - c))

    half = ket_transform(pair_ints, occ_lam, occ_sig, slabs)
    owned = lax.all_to_all(half, "ao", split_axis=0, concat_axis=0, tiled=True)
    chunk = lax.dynamic_slice_in_dim(coef_act, ao_index * 256, 256, 0)
    with jax.named_scope("s_c1"):
        row = jnp.stack(direct(chunk, 0))
    with jax.named_scope("s_c2"):
        whole = jnp.concatenate(direct(row, 1), axis=0)
    with jax.named_scope("s_p1"):
        near = direct(owned, 0)
        near_first, near_second = [
            jnp.concatenate([piece[:, k] for piece in near], axis=0) for k in range(2)
        ]
    with jax.named_scope("s_p2a"):
        first = both_ways(near_first, up, down)
    plan = plan_terms(after(shell_pairs, half), place)
    with jax.named_scope("s_z1"):
        column = both_ways(after(whole, near_first, plan), z_up, z_down)
    with jax.named_scope("s_p2b"):
        second = both_ways(after(near_second, *first), up, down)
    with jax.named_scope("s_f2a"):
        first += far_halves(first, up, down)
    with jax.named_scope("s_zf"):
        column += far_halves(column, z_up, z_down, *first[3:])
    left = left_of_slab(plan, first, coef_act)
    with jax.named_scope("s_f2b"):
        second += far_halves(second, up, down, left)
    with jax.named_scope("s_swap"):
        pieces = list(column) + [send(after(piece, first[4]), swap) for piece in column]
    out = finish(plan, place, second, coef_act, pieces, left)
    return out.reshape(2, 1, NI, PANEL, ACT)


def solution(mesh):
    return jax.shard_map(
        body,
        mesh=mesh,
        in_specs=(P(("ao", "mo"), None, None), P(), P(), P(), P(None, "mo"), P()),
        out_specs=P(None, "ao", None, "mo", None),
        check_vma=False,
    )
```

```python
import functools

import jax
import jax.numpy as jnp
from jax import lax
from jax.experimental import pallas as pl
from jax.experimental.pallas import tpu as pltpu
from jax.sharding import PartitionSpec as P

SH = 64
NSH = 32
NAO = 2048
ACT = 2048
KL = 16
KS = 16
NI = 4
NJ = 8
NOCC = 32
NBLK = 128
PANEL = 128
ROWS = NI * PANEL
VMEM_LIMIT = 60 << 20
AXES = ("ao", "mo")


def device_pairs(move):
    pairs = []
    for z in range(4):
        for c in range(2):
            for x in range(4):
                for y in range(4):
                    x2, y2, z2, c2 = move(x, y, z, c)
                    source = (z * 2 + c) * 16 + x * 4 + y
                    target = ((z2 % 4) * 2 + c2) * 16 + (x2 % 4) * 4 + y2 % 4
                    pairs.append((source, target))
    return pairs


def plane_pairs(step, phase):
    return device_pairs(
        lambda x, y, z, c: (x + step, y, z, c) if c == phase else (x, y + step, z, c)
    )


def z_pairs(step):
    return device_pairs(lambda x, y, z, c: (x, y, z + step, c))


def send(value, pairs):
    return lax.ppermute(value, AXES, pairs)


def after(value, *others):
    return lax.optimization_barrier((value, *others))[0]


def both_ways(value, pairs_up, pairs_down):
    return value, send(value, pairs_up), send(value, pairs_down)


def far_halves(pieces, pairs_up, pairs_down, *others):
    half = pieces[0].shape[0] // 2
    return (
        send(after(pieces[1], *others)[:half], pairs_up),
        send(after(pieces[2], *others)[half:], pairs_down),
    )


def direct(value, phase):
    return [value] + [send(value, plane_pairs(step, phase)) for step in (1, -1, 2)]


def ket_kernel(slabs_ref, lam_ref, sig_ref, ints_hbm, out_ref, ints, wide, sems):
    copies = [
        pltpu.make_async_copy(
            ints_hbm.at[0, pl.ds(n * 1024, 1024)], ints.at[pl.ds(n * 1024, 1024)], sems.at[n]
        )
        for n in range(4)
    ]
    for copy in copies:
        copy.start()
    rows = lax.broadcasted_iota(jnp.int32, (64, NOCC), 0)
    column = lax.broadcasted_iota(jnp.int32, (64, NOCC), 1)
    number = jnp.where((rows & 1) == 0, slabs_ref[0], slabs_ref[1]) * NI + (rows >> 4)
    pick_lam = jnp.where(column == number, 1.0, 0.0).astype(jnp.bfloat16)
    rows = lax.broadcasted_iota(jnp.int32, (64, NJ), 0)
    column = lax.broadcasted_iota(jnp.int32, (64, NJ), 1)
    pick_sig = jnp.where(column == ((rows >> 1) & 7), 1.0, 0.0).astype(jnp.bfloat16)
    line = lax.broadcasted_iota(jnp.int32, (KL, KL * KS), 0)
    word = lax.broadcasted_iota(jnp.int32, (KL, KL * KS), 1)
    spread_lam = jnp.where((word >> 4) == line, 1.0, 0.0).astype(jnp.bfloat16)
    spread_sig = jnp.where((word & 15) == line, 1.0, 0.0).astype(jnp.bfloat16)

    few_lam = lax.dot_general(
        pick_lam, lam_ref[...], (((1,), (1,)), ((), ())), preferred_element_type=jnp.float32
    )
    few_sig = jnp.dot(pick_sig, sig_ref[...], preferred_element_type=jnp.float32)

    def spread_out(few, spread):
        return jnp.dot(few.astype(jnp.bfloat16), spread, preferred_element_type=jnp.float32)

    pair_coef = spread_out(few_lam, spread_lam) * spread_out(few_sig, spread_sig)
    pair_coef = pair_coef.astype(jnp.bfloat16)
    low = lax.broadcasted_iota(jnp.int32, (16, 128), 1) < SH
    for n in range(4):
        copies[n].wait()
        for part in range(2):
            first = n * 1024 + part * 512
            result = lax.dot_general(
                pair_coef, ints[first:first + 512, :], (((1,), (1,)), ((), ())),
                preferred_element_type=jnp.float32,
            )
            for t in range(4):
                mu = first // SH + 2 * t
                for ip in range(2):
                    even = result[ip * 32:ip * 32 + 16, t * 128:t * 128 + 128]
                    odd = result[ip * 32 + 16:ip * 32 + 32, t * 128:t * 128 + 128]
                    lanes = slice(ip * 128, ip * 128 + 128)
                    wide[ip, pl.ds(mu, 16, stride=SH), :] = jnp.where(low, even, pltpu.roll(odd, SH, 1))
                    wide[ip, pl.ds(mu + 1, 16, stride=SH), :] = jnp.where(low, pltpu.roll(even, SH, 1), odd)
    for ip in range(2):
        out_ref[:, ip * 128:ip * 128 + 128] = wide[ip].astype(jnp.bfloat16)


def ket_transform(pair_ints, occ_lam, occ_sig, slabs):
    out = pl.pallas_call(
        ket_kernel,
        out_shape=jax.ShapeDtypeStruct((NJ * 2 * SH, NI * SH), jnp.bfloat16),
        in_specs=[
            pl.BlockSpec(memory_space=pltpu.SMEM),
            pl.BlockSpec(memory_space=pltpu.VMEM),
            pl.BlockSpec(memory_space=pltpu.VMEM),
            pl.BlockSpec(memory_space=pltpu.HBM),
        ],
        out_specs=pl.BlockSpec(memory_space=pltpu.VMEM),
        scratch_shapes=[
            pltpu.VMEM((SH * SH, KL * KS), jnp.bfloat16),
            pltpu.VMEM((2, NJ * 2 * SH, 128), jnp.float32),
            pltpu.SemaphoreType.DMA((4,)),
        ],
        compiler_params=pltpu.CompilerParams(vmem_limit_bytes=VMEM_LIMIT),
        cost_estimate=pl.CostEstimate(flops=140_000_000, bytes_accessed=3_000_000, transcendentals=0),
        name="ket_transform",
    )(slabs, occ_lam, occ_sig.T, pair_ints)
    return out.reshape(NJ, 2, SH, NI * SH)


def ring_place(offset):
    return jnp.where(offset == 0, 0, jnp.where(offset == 3, 1, offset + 1))


def ring_offset(place):
    return jnp.where(place == 0, 0, jnp.where(place == 3, 2, (place * 2 + 1) & 3))


def plan_kernel(place_ref, pairs_ref, across_ref, plan_ref):
    x = place_ref[0]
    y = place_ref[1]
    core = place_ref[3]
    size = (NBLK, NBLK)
    row = lax.broadcasted_iota(jnp.int32, size, 0)
    lane = lax.broadcasted_iota(jnp.int32, size, 1)
    p = row[:, 0:1]
    away_x = (((p >> 2) & 3) - x) & 3
    away_y = ((p & 3) - y) & 3
    inner = ring_place(jnp.where(core == 0, away_x, away_y))
    outer = ring_place(jnp.where(core == 0, away_y, away_x))
    slot = (outer * 4 + inner) * 8 + (p >> 4)
    wide = lax.broadcasted_iota(jnp.int32, (NBLK, 2 * NBLK), 1)

    def total(mask, value, axis):
        picked = jnp.where(mask, value.astype(jnp.float32), 0.0)
        return jnp.sum(picked, axis=axis, keepdims=True).astype(jnp.int32)

    one_down = pairs_ref[:, 0:1]
    two_down = pairs_ref[:, 1:2]
    one_across = across_ref[0:1, :]
    two_across = across_ref[1:2, :]
    lines = []
    targets = []
    for kind in range(2):
        if kind == 0:
            down, across, other = two_down, two_across, one_down
        else:
            other = two_down
            down = jnp.where(one_down == two_down, NBLK - 1, one_down)
            across = jnp.where(one_across == two_across, NBLK - 1, one_across)
        ones = jnp.ones(size, jnp.int32)
        rank = total((down == across) & (lane < row), ones, 1)
        groups_across = jnp.where(lane[0:1] < NSH, (total(down == lane, ones, 0) + 3) >> 2, 0)
        groups_down = jnp.where(row[:, 0:1] < NSH, (total(across == row, ones, 1) + 3) >> 2, 0)
        groups_square = jnp.broadcast_to(groups_across, size)
        before_term = total(lane < down, groups_square, 1)
        before_shell = total(lane < row, groups_square, 1)
        position = jnp.where(down < NSH, before_term * 4 + rank, -1)
        entry = jnp.broadcast_to(other * 256 + slot - NBLK, wide.shape)
        lines.append(total(position == wide, entry, 0) + NBLK)
        here = (lane >= before_shell) & (lane < before_shell + groups_down)
        shell = total(here, row - NSH, 0) + NSH
        number = jnp.sum(groups_across.astype(jnp.float32), axis=1, keepdims=True).astype(jnp.int32)
        targets.append(jnp.concatenate([shell, jnp.broadcast_to(number, shell.shape)], axis=1))
    plan_ref[...] = jnp.concatenate(lines + targets + lines + targets, axis=0)


def plan_terms(shell_pairs, place):
    return pl.pallas_call(
        plan_kernel,
        out_shape=jax.ShapeDtypeStruct((8, 2 * NBLK), jnp.int32),
        in_specs=[
            pl.BlockSpec(memory_space=pltpu.SMEM),
            pl.BlockSpec(memory_space=pltpu.VMEM),
            pl.BlockSpec(memory_space=pltpu.VMEM),
        ],
        out_specs=pl.BlockSpec(memory_space=pltpu.VMEM),
        compiler_params=pltpu.CompilerParams(vmem_limit_bytes=VMEM_LIMIT),
        cost_estimate=pl.CostEstimate(flops=2_000_000, bytes_accessed=10_000, transcendentals=0),
        name="plan_terms",
    )(place, shell_pairs, shell_pairs.T)


UNROLL = 14
FIRSTS = (0, 32, 64, 96, 112, 128)


def build_left(plan_ref, halves, panel_hbm, left, scratch, start_others=lambda: None):
    blocks, panel, lhs, acc, sem_blocks, sem_panel = scratch
    copy_panel = pltpu.make_async_copy(panel_hbm, panel, sem_panel)
    copy_panel.start()
    copies = [
        pltpu.make_async_copy(
            halves[i], blocks.at[pl.ds(FIRSTS[i], FIRSTS[i + 1] - FIRSTS[i])], sem_blocks.at[i]
        )
        for i in range(5)
    ]
    for copy in copies:
        copy.start()
    others = start_others()
    blocks[NBLK] = jnp.zeros(blocks.shape[1:], jnp.bfloat16)

    @pl.loop(0, NSH)
    def _(shell):
        acc[shell] = jnp.zeros(acc.shape[1:], jnp.float32)

    copy_panel.wait()
    for shell in range(NSH):
        rows = panel[shell * SH:(shell + 1) * SH, :]
        lhs[shell] = jnp.concatenate([rows, rows], axis=0).T
    low = lax.broadcasted_iota(jnp.int32, (PANEL, 128), 1) < SH
    low_rows = lax.broadcasted_iota(jnp.int32, (SH, 128), 1) < SH
    for copy in copies:
        copy.wait()

    def terms(kind, group):
        entries = [plan_ref[kind, group * 4 + k] for k in range(4)]
        target = plan_ref[2 + kind, group]
        factor = jnp.concatenate(
            [
                jnp.where(low, lhs[entries[2 * h] >> 8], lhs[entries[2 * h + 1] >> 8])
                for h in range(2)
            ],
            axis=1,
        )
        values = [blocks[entry & 255] for entry in entries]
        if kind == 0:
            return target, jnp.dot(
                factor, jnp.concatenate(values, axis=0), preferred_element_type=jnp.float32
            )
        columns = []
        for h in range(2):
            stack = []
            for rp in range(2):
                a = values[2 * h][:, rp * 128:rp * 128 + 128]
                b = values[2 * h + 1][:, rp * 128:rp * 128 + 128]
                stack.append(jnp.where(low_rows, a, pltpu.roll(b, SH, 1)))
                stack.append(jnp.where(low_rows, pltpu.roll(a, SH, 1), b))
            columns.append(jnp.concatenate(stack, axis=0))
        return target, lax.dot_general(
            factor, jnp.concatenate(columns, axis=1), (((1,), (1,)), ((), ())),
            preferred_element_type=jnp.float32,
        )

    most = jnp.maximum(plan_ref[2, NBLK], plan_ref[3, NBLK])

    @pl.loop(0, (most + UNROLL - 1) // UNROLL)
    def _(step):
        for u in range(UNROLL):
            for kind in range(2):
                target, sums = terms(kind, step * UNROLL + u)
                acc[target] += sums

    @pl.loop(0, NSH // 2, unroll=8)
    def _(t):
        for rp in range(2):
            even = acc[2 * t, :, rp * 128:rp * 128 + 128]
            odd = acc[2 * t + 1, :, rp * 128:rp * 128 + 128]
            columns = pl.ds(pl.multiple_of(t * 128, 128), 128)
            left[rp * 2 * PANEL:(rp * 2 + 1) * PANEL, columns] = jnp.where(
                low, even, pltpu.roll(odd, SH, 1)
            ).astype(jnp.bfloat16)
            left[(rp * 2 + 1) * PANEL:(rp * 2 + 2) * PANEL, columns] = jnp.where(
                low, pltpu.roll(even, SH, 1), odd
            ).astype(jnp.bfloat16)
    return others


LEFT_SCRATCH = [
    pltpu.VMEM((NBLK + 1, SH, NI * SH), jnp.bfloat16),
    pltpu.VMEM((NAO, PANEL), jnp.bfloat16),
    pltpu.VMEM((NSH, PANEL, 2 * SH), jnp.bfloat16),
    pltpu.VMEM((NSH + 1, PANEL, NI * SH), jnp.float32),
    pltpu.SemaphoreType.DMA((5,)),
    pltpu.SemaphoreType.DMA,
]


def start_coefs(place_ref, pieces, coefs, sems):
    z = place_ref[2]
    core = place_ref[3]
    copies = []
    for k in range(10):
        offset = (0, 3, 1, 2, 2)[k % 5]
        base, slots = ((0, 16), (0, 16), (0, 16), (0, 8), (8, 8))[k % 5]
        chunk = ((z + offset) & 3) * 2 + (core if k < 5 else 1 - core)
        copies.append(
            pltpu.make_async_copy(pieces[k], coefs.at[chunk, pl.ds(base, slots)], sems.at[k])
        )
    for copy in copies:
        copy.start()
    return copies


def multiply(place_ref, left, coefs, out_ref, staged, sem_out):
    x = place_ref[0]
    y = place_ref[1]

    def slot_of(panel, which_core):
        there = (panel >> 2, panel & 3)
        first = (there[0] - x) & 3
        second = (there[1] - y) & 3
        if which_core == 1:
            first, second = second, first
        return ring_place(second) * 4 + ring_place(first)

    def out_copy(n, slot):
        return pltpu.make_async_copy(
            staged.at[slot],
            out_ref.at[:, :, pl.ds(pl.multiple_of(n * 256, 256), 256)],
            sem_out.at[slot],
        )

    @pl.loop(0, ACT // 256, unroll=4)
    def _(n):
        slot = n % 2

        @pl.when(n >= 2)
        def _():
            out_copy(n - 2, slot).wait()

        slots = [[slot_of(2 * n + h, c) for h in range(2)] for c in range(2)]
        rhs = jnp.concatenate(
            [
                jnp.concatenate([coefs[chunk, slots[chunk % 2][h]] for h in range(2)], axis=1)
                for chunk in range(8)
            ],
            axis=0,
        )
        for slab in range(2):
            product = jnp.dot(left[slab], rhs, preferred_element_type=jnp.float32)
            staged[slot, slab] = product.astype(jnp.bfloat16)
        out_copy(n, slot).start()

    out_copy(ACT // 256 - 2, 0).wait()
    out_copy(ACT // 256 - 1, 1).wait()


def left_kernel(*refs):
    build_left(refs[0], refs[1:6], refs[6], refs[7], refs[8:])


def left_of_slab(plan, halves, panel):
    return pl.pallas_call(
        left_kernel,
        out_shape=jax.ShapeDtypeStruct((ROWS, NAO), jnp.bfloat16),
        in_specs=[pl.BlockSpec(memory_space=pltpu.SMEM)] + [pl.BlockSpec(memory_space=pltpu.HBM)] * 6,
        out_specs=pl.BlockSpec(memory_space=pltpu.VMEM),
        scratch_shapes=LEFT_SCRATCH,
        compiler_params=pltpu.CompilerParams(vmem_limit_bytes=16 << 20),
        cost_estimate=pl.CostEstimate(flops=9_000_000_000, bytes_accessed=7_000_000, transcendentals=0),
        name="left_of_slab",
    )(plan, *halves, panel)


def finish_kernel(*refs):
    plan_ref, place_ref = refs[:2]
    out_ref, coefs, left, staged, sem_coefs, sem_out, sem_left = refs[19:26]

    def start_others():
        copy_left = pltpu.make_async_copy(refs[18], left.at[0], sem_left)
        copy_left.start()
        return [copy_left] + start_coefs(place_ref, refs[8:18], coefs, sem_coefs)

    copies = build_left(plan_ref, refs[2:7], refs[7], left.at[1], refs[26:], start_others)
    for copy in copies:
        copy.wait()
    multiply(place_ref, left, coefs, out_ref, staged, sem_out)


def finish(plan, place, halves, panel, pieces, left):
    return pl.pallas_call(
        finish_kernel,
        out_shape=jax.ShapeDtypeStruct((2, ROWS, ACT), jnp.bfloat16),
        in_specs=[pl.BlockSpec(memory_space=pltpu.SMEM)] * 2 + [pl.BlockSpec(memory_space=pltpu.HBM)] * 17,
        out_specs=pl.BlockSpec(memory_space=pltpu.HBM),
        scratch_shapes=[
            pltpu.VMEM((8, 16, 256, PANEL), jnp.bfloat16),
            pltpu.VMEM((2, ROWS, NAO), jnp.bfloat16),
            pltpu.VMEM((2, 2, ROWS, 256), jnp.bfloat16),
            pltpu.SemaphoreType.DMA((10,)),
            pltpu.SemaphoreType.DMA((2,)),
            pltpu.SemaphoreType.DMA,
        ] + LEFT_SCRATCH,
        compiler_params=pltpu.CompilerParams(vmem_limit_bytes=28 << 20),
        cost_estimate=pl.CostEstimate(flops=18_000_000_000, bytes_accessed=20_000_000, transcendentals=0),
        name="finish",
    )(plan, place, *halves, panel, *pieces, left)


def body(pair_ints, shell_pairs, occ_lam, occ_sig, coef_act, slabs):
    ao_index = lax.axis_index("ao")
    mo_index = lax.axis_index("mo")
    place = jnp.stack([mo_index >> 2, mo_index & 3, ao_index >> 1, ao_index & 1]).astype(jnp.int32)

    up, down = plane_pairs(1, 1), plane_pairs(-1, 1)
    z_up, z_down = z_pairs(1), z_pairs(-1)
    swap = device_pairs(lambda x, y, z, c: (x, y, z, 1 - c))

    half = ket_transform(pair_ints, occ_lam, occ_sig, slabs)
    owned = lax.all_to_all(half, "ao", split_axis=0, concat_axis=0, tiled=True)
    chunk = lax.dynamic_slice_in_dim(coef_act, ao_index * 256, 256, 0)
    with jax.named_scope("s_c1"):
        row = jnp.stack(direct(chunk, 0))
    with jax.named_scope("s_c2"):
        whole = jnp.concatenate(direct(row, 1), axis=0)
    with jax.named_scope("s_p1"):
        near = direct(owned, 0)
        near_first, near_second = [
            jnp.concatenate([piece[:, k] for piece in near], axis=0) for k in range(2)
        ]
    with jax.named_scope("s_p2a"):
        first = both_ways(near_first, up, down)
    plan = plan_terms(after(shell_pairs, half), place)
    with jax.named_scope("s_z1"):
        column = both_ways(after(whole, near_first, plan), z_up, z_down)
    with jax.named_scope("s_p2b"):
        second = both_ways(after(near_second, *first), up, down)
    with jax.named_scope("s_f2a"):
        first += far_halves(first, up, down)
    with jax.named_scope("s_zf"):
        column += far_halves(column, z_up, z_down, *first[3:])
    left = left_of_slab(plan, first, coef_act)
    with jax.named_scope("s_f2b"):
        second += far_halves(second, up, down, left)
    with jax.named_scope("s_swap"):
        pieces = list(column) + [send(after(piece, first[4]), swap) for piece in column]
    out = finish(plan, place, second, coef_act, pieces, left)
    return out.reshape(2, 1, NI, PANEL, ACT)


def solution(mesh):
    return jax.shard_map(
        body,
        mesh=mesh,
        in_specs=(P(("ao", "mo"), None, None), P(), P(), P(), P(None, "mo"), P()),
        out_specs=P(None, "ao", None, "mo", None),
        check_vma=False,
    )
```
